512 devices in a mesh: outer: 16 (over z_hi, x, core), inner: 32 (over z_lo, y).
Axes of the slice: x: 4, y: 8, z: 8 (z_hi: 2, z_lo: 4; z = z_hi * 4 + z_lo), core: 2. Of those that a mesh axis runs over, the one named last changes fastest.
Arguments:
- diag_blocks: float32 [65536, 128], P(('outer', 'inner')), may hold values from -24 to 25, as said below
- left_bases: float32 [9, 65536, 128], P(None, ('outer', 'inner')), may hold values from -6 to 6
- right_bases: float32 [9, 65536, 128], P(None, ('outer', 'inner')), may hold values from -0.0625 to 0.0625, as said below
- sources: float32 [65536, 128], P(('outer', 'inner')), may hold values from -6 to 6
Outputs:
- updated_bases: float32 [9, 65536, 128], P(None, ('outer', 'inner'))
- solution: float32 [65536, 128], P(('outer', 'inner'))
The draws below stay inside these ranges and needn't reach their ends.
Inputs may be any that keep to these rules, and one draw needn't show every extreme that they name: `diag_blocks`: each leaf block is symmetric with all eigenvalues 1 or more. `right_bases`: the row bases of level l have entries within 8 / (128 * 2 ** (l - 1)) of zero.
All inputs are finite; a program needn't handle non-finite values.
Results may differ from the reference program's by a relative error of at most 0.0001.
Values sent between devices are 32-bit elements; how exact they have to be, the bound alone decides.
No kernel may reach another device: no remote copies, remote signals or barrier semaphores. Data moves between devices by JAX's collectives and lax.ppermute only.
A program may use at most 64 MiB of HBM per device.

```python
import jax
import jax.numpy as jnp
from jax import lax

RANK = 128
RHS = 128
ROWS_DEV = 128
NROWS = 65536
LEVELS = 9


def common_draw(key):
    blocks = NROWS // ROWS_DEV
    base = jax.random.fold_in(key, 101)
    keys = jax.random.split(base, 4)
    factor_raw = jnp.clip(jax.random.normal(keys[0], (blocks, ROWS_DEV, ROWS_DEV), jnp.float32), -4.0, 4.0)
    column_raw = jax.random.normal(keys[1], (LEVELS, blocks, ROWS_DEV, RANK), jnp.float32)
    noise = jax.random.normal(keys[3], (LEVELS, blocks, ROWS_DEV, RANK), jnp.float32)
    column = jnp.clip(column_raw, -6.0, 6.0)
    gram = jnp.einsum('bik,bjk->bij', factor_raw, factor_raw, precision=lax.Precision.HIGHEST) / ROWS_DEV
    gram = 0.5 * (gram + jnp.swapaxes(gram, 1, 2))
    leaf = jnp.eye(ROWS_DEV, dtype=jnp.float32)[None] + 1.5 * gram
    applied = jnp.einsum('bij,lbjr->lbir', leaf, column, precision=lax.Precision.HIGHEST)
    level_ids = jnp.arange(LEVELS).astype(jnp.int32)
    block_ids = jnp.arange(blocks).astype(jnp.int32)
    side = jnp.right_shift(block_ids[None, :], level_ids[:, None]) & 1
    sign = (1 - 2 * side).astype(jnp.float32)
    half = ROWS_DEV * jnp.exp2(level_ids.astype(jnp.float32))
    structured = sign[:, :, None, None] * (0.5 / half)[:, None, None, None] * applied
    rough = (0.04 / jnp.sqrt(half))[:, None, None, None] * noise
    limit = (8.0 / half)[:, None, None, None]
    rowbasis = jnp.clip(structured + rough, -limit, limit)
    return (leaf.reshape(NROWS, ROWS_DEV), column.reshape(LEVELS, NROWS, RANK), rowbasis.reshape(LEVELS, NROWS, RANK))


def draw_diag_blocks(key, part):
    return common_draw(key)[0]


def draw_left_bases(key, part):
    return common_draw(key)[1]


def draw_right_bases(key, part):
    return common_draw(key)[2]


def levels(rng, extent, cuts, low, largest):
    def one(dim, parts):
        heights = jax.random.uniform(jax.random.fold_in(jax.random.fold_in(rng, 6), dim), (parts,), jnp.float32, low / len(cuts), largest / len(cuts))
        return jnp.repeat(jnp.exp(heights), extent[dim] // parts).reshape((-1,) + (1,) * (len(extent) - dim - 1))

    gain = one(*cuts[0])
    for cut in cuts[1:]:
        gain = gain * one(*cut)
    return gain


def bell_draw(rng, extent, scale, reach, pieces=(), kind=jnp.bfloat16):
    values = jax.random.normal(rng, extent, jnp.float32) * scale
    if len(pieces) > 0:
        values = levels(rng, extent, pieces, -0.22, 0.18) * values
    return jnp.clip(values, min=-reach, max=reach).astype(kind)


def setup_inputs(seed: int = 0) -> dict:
    key_list = jax.random.split(jax.random.key(seed), 5)
    return {
        "diag_blocks": draw_diag_blocks(jax.random.fold_in(key_list[4], 71), 0),
        "left_bases": draw_left_bases(jax.random.fold_in(key_list[4], 71), 0),
        "right_bases": draw_right_bases(jax.random.fold_in(key_list[4], 71), 0),
        "sources": bell_draw(key_list[3], (NROWS, RHS), 1.0, 6.0, ((0, 512),), jnp.float32),
    }


HI = lax.Precision.HIGHEST

def solve_lower(factor, target, transpose):
    return lax.linalg.triangular_solve(factor, target, left_side=True, lower=True, transpose_a=transpose)

def leaf_solve(factor, target):
    blocks = factor.shape[0]
    rhs = target.reshape(blocks, ROWS_DEV, target.shape[1])
    inner_sol = solve_lower(factor, rhs, False)
    return solve_lower(factor, inner_sol, True).reshape(NROWS, target.shape[1])

def reference(diag_blocks, left_bases, right_bases, sources):
    blocks = diag_blocks.reshape(NROWS // ROWS_DEV, ROWS_DEV, ROWS_DEV)
    factor = jnp.linalg.cholesky(blocks)
    targets = [leaf_solve(factor, left_bases[level]) for level in range(LEVELS)]
    targets.append(leaf_solve(factor, sources))
    for level in range(LEVELS):
        half = ROWS_DEV * 2 ** level
        pairs = NROWS // (2 * half)
        vpart = right_bases[level].reshape(pairs, 2, half, RANK)
        wpart = targets[level].reshape(pairs, 2, half, RANK)
        gram = jnp.einsum('gsnr,gsnc->gsrc', vpart, wpart, precision=HI)
        lower_g = gram[:, 0]
        upper_g = gram[:, 1]
        eye = jnp.eye(RANK, dtype=jnp.float32)
        matrix = eye - jnp.einsum('grk,gkc->grc', lower_g, upper_g, precision=HI)
        normal = jnp.einsum('gkr,gkc->grc', matrix, matrix, precision=HI)
        chol = jnp.linalg.cholesky(normal)
        for later in range(level + 1, LEVELS + 1):
            width = targets[later].shape[1]
            block = targets[later].reshape(pairs, 2, half, width)
            proj = jnp.einsum('gsnr,gsnc->gsrc', vpart, block, precision=HI)
            lower_p = proj[:, 0]
            upper_p = proj[:, 1]
            right = lower_p - jnp.einsum('grk,gkc->grc', lower_g, upper_p, precision=HI)
            right = jnp.einsum('gkr,gkc->grc', matrix, right, precision=HI)
            first = solve_lower(chol, right, False)
            upper_y = solve_lower(chol, first, True)
            lower_y = upper_p - jnp.einsum('grk,gkc->grc', upper_g, upper_y, precision=HI)
            coef = jnp.stack([lower_y, upper_y], axis=1)
            block = block - jnp.einsum('gsnr,gsrc->gsnc', wpart, coef, precision=HI)
            targets[later] = block.reshape(NROWS, width)
    return (jnp.stack(targets[:LEVELS], axis=0), targets[LEVELS])
```

```python
import jax
import jax.numpy as jnp
from jax import lax
from jax.experimental import pallas as pl
from jax.experimental.pallas import tpu as pltpu
from jax.sharding import Mesh, PartitionSpec as P

HI = lax.Precision.HIGHEST
BITS = 9
NAMES = tuple("b%d" % bit for bit in reversed(range(BITS)))
TOP = 5
N = 128


def axes(low, high):
    return tuple("b%d" % bit for bit in reversed(range(low, high)))


def dot(a, b):
    return jnp.dot(a, b, precision=HI, preferred_element_type=jnp.float32)


def tdot(a, b):
    return lax.dot_general(a, b, (((0,), (0,)), ((), ())), precision=HI, preferred_element_type=jnp.float32)


def quick(a, b):
    return jnp.dot(a.astype(jnp.bfloat16), b.astype(jnp.bfloat16), preferred_element_type=jnp.float32)


def eye():
    row = lax.broadcasted_iota(jnp.int32, (N, N), 0)
    col = lax.broadcasted_iota(jnp.int32, (N, N), 1)
    return (row == col).astype(jnp.float32)


def wide(ref, first, last):
    return jnp.concatenate([ref[i] for i in range(first, last)], axis=1)


def invert(matrix, start, rounds, out_ref):
    one = eye()
    value = start
    for _ in range(rounds):
        value = value + quick(value, one - quick(matrix, value))
    for _ in range(2):
        rest = one - dot(matrix, value)
        value = value + quick(value, rest)
    out_ref[...] = value
    left = jnp.sum(rest * rest)

    @pl.when(jnp.logical_not(left < 1e-6))
    def _():
        out_ref[...] = start

        def more(state):
            step, left = state
            return jnp.logical_and(step < 60, jnp.logical_not(left < 1e-9))

        def body(state):
            step, _ = state
            now = out_ref[...]
            rest = eye() - dot(matrix, now)
            out_ref[...] = now + dot(now, rest)
            return step + 1, jnp.sum(rest * rest)

        lax.while_loop(more, body, (jnp.int32(0), jnp.float32(1.0)))


def general_start(matrix):
    size = jnp.abs(matrix)
    by_col = jnp.max(jnp.sum(size, axis=0, keepdims=True), axis=1, keepdims=True)
    by_row = jnp.max(jnp.sum(size, axis=1, keepdims=True), axis=0, keepdims=True)
    return matrix.T * (1.9 / (by_col * by_row))


def leaf_kernel(diag_ref, left_ref, right_ref, source_ref, work_ref, panel_ref, inv_ref):
    levels = left_ref.shape[0]
    diag = diag_ref[...]
    bound = jnp.max(jnp.sum(jnp.abs(diag), axis=0, keepdims=True), axis=1, keepdims=True)
    invert(diag, eye() * (2.0 / (1.0 + bound)), 6, inv_ref)
    rhs = jnp.concatenate([left_ref[i] for i in range(levels)] + [source_ref[...]], axis=1)
    work = dot(inv_ref[...], rhs)
    panel = tdot(right_ref[...], work)
    for i in range(levels + 1):
        work_ref[i] = work[:, i * N : (i + 1) * N]
        panel_ref[i] = panel[:, i * N : (i + 1) * N]


def own_coef(own_ref, other_ref, count, inv_ref):
    own_g = own_ref[0]
    other_g = other_ref[0]
    matrix = eye() - dot(other_g, own_g)
    invert(matrix, general_start(matrix), 7, inv_ref)
    own_p = wide(own_ref, 1, count)
    right = wide(other_ref, 1, count) - dot(other_g, own_p)
    return dot(inv_ref[...], right)


def level_kernel(level, count, own_ref, other_ref, work_ref, right_ref, next_ref, panel_ref, inv_ref):
    coef = own_coef(own_ref, other_ref, count, inv_ref)
    later = wide(work_ref, level + 1, level + count) - dot(work_ref[level], coef)
    for i in range(level + 1):
        next_ref[i] = work_ref[i]
    for i in range(count - 1):
        next_ref[level + 1 + i] = later[:, i * N : (i + 1) * N]
    rows = right_ref.shape[0]
    for k in range(rows):
        panel = tdot(right_ref[k], later)
        for i in range(count - 1):
            panel_ref[k * (count - 1) + i] = panel[:, i * N : (i + 1) * N]


def front_kernel(count, own_ref, other_ref, coef_ref, front_ref, inv_ref):
    coef = own_coef(own_ref, other_ref, count, inv_ref)
    for i in range(count - 1):
        coef_ref[i] = coef[:, i * N : (i + 1) * N]
    other_coef = wide(own_ref, 1, count) - dot(own_ref[0], coef)
    for k in range(1, count - 1):
        base = k * count
        total = wide(own_ref, base + 1, base + count) + wide(other_ref, base + 1, base + count)
        total = total - dot(own_ref[base], coef) - dot(other_ref[base], other_coef)
        for i in range(count - 1):
            front_ref[(k - 1) * (count - 1) + i] = total[:, i * N : (i + 1) * N]


def last_front_kernel(count, own_ref, other_ref, coef_ref, inv_ref):
    coef_ref[0] = own_coef(own_ref, other_ref, count, inv_ref)


def apply_kernel(level, count, work_ref, coef_ref, next_ref):
    coef = wide(coef_ref, 0, count - 1)
    later = wide(work_ref, level + 1, level + count) - dot(work_ref[level], coef)
    for i in range(level + 1):
        next_ref[i] = work_ref[i]
    for i in range(count - 1):
        next_ref[level + 1 + i] = later[:, i * N : (i + 1) * N]


def blocks(count):
    return jax.ShapeDtypeStruct((count, N, N), jnp.float32)


def call(body, name, outs, *args, scratch=True):
    return pl.pallas_call(
        body,
        out_shape=outs,
        scratch_shapes=[pltpu.VMEM((N, N), jnp.float32)] if scratch else [],
        name=name,
    )(*args)


def partner(value, bit):
    return lax.ppermute(value, "b%d" % bit, [(0, 1), (1, 0)])


def exchange(value, names):
    return lax.all_to_all(value, names, 0, 0)


def half_sums(panel, level):
    count = panel.shape[0]
    size = 2 ** (level + 1)
    rows = count * N // size
    names = axes(0, level + 1)
    pieces = exchange(panel.reshape(size, rows, N), names)
    sums = pieces.reshape(2, size // 2, rows, N).sum(axis=1)
    both = exchange(jnp.broadcast_to(sums[None], (size, 2, rows, N)), names)
    return both[:, 0].reshape(count, N, N), both[:, 1].reshape(count, N, N)


def total(panel, level):
    count = panel.shape[0]
    size = 2**level
    rows = count * N // size
    names = axes(0, level)
    pieces = exchange(panel.reshape(size, rows, N), names)
    part = pieces.sum(axis=0)
    return exchange(jnp.broadcast_to(part[None], (size, rows, N)), names).reshape(count, N, N)


def per_device(diag_blocks, left_bases, right_bases, sources):
    levels = left_bases.shape[0]
    targets = levels + 1
    work, panel = call(leaf_kernel, "leaf", (blocks(targets), blocks(targets)), diag_blocks, left_bases, right_bases[0], sources)
    for level in range(TOP):
        count = targets - level
        if level == 0:
            own, other = panel, partner(panel, 0)
        else:
            lower, upper = half_sums(panel, level)
            is_lower = lax.axis_index("b%d" % level) == 0
            own = jnp.where(is_lower, lower, upper)
            other = jnp.where(is_lower, upper, lower)
        rows = 1 if level + 1 < TOP else levels - TOP

        def body(*refs, level=level, count=count):
            level_kernel(level, count, *refs)

        work, panel = call(
            body,
            "level%d" % level,
            (blocks(targets), blocks(rows * (count - 1))),
            own,
            other,
            work,
            right_bases[level + 1 : level + 1 + rows],
        )
    front = total(panel, TOP)
    for level in range(TOP, levels):
        count = targets - level
        other = partner(front, level)
        if level + 1 < levels:

            def body(*refs, count=count):
                front_kernel(count, *refs)

            coef, front = call(body, "front%d" % level, (blocks(count - 1), blocks((count - 2) * (count - 1))), front, other)
        else:

            def body(*refs, count=count):
                last_front_kernel(count, *refs)

            coef = call(body, "front%d" % level, blocks(1), front, other)

        def apply(*refs, level=level, count=count):
            apply_kernel(level, count, *refs)

        work = call(apply, "apply%d" % level, blocks(targets), work, coef, scratch=False)
    return work[:levels], work[levels]


def solution(mesh):
    fine = Mesh(mesh.devices.reshape((2,) * BITS), NAMES)
    rows = P(NAMES, None)
    stacked = P(None, NAMES, None)
    return jax.shard_map(
        per_device,
        mesh=fine,
        in_specs=(rows, stacked, stacked, rows),
        out_specs=(stacked, rows),
        check_vma=False,
    )
```

```python
import jax
import jax.numpy as jnp
from jax import lax
from jax.experimental import pallas as pl
from jax.experimental.pallas import tpu as pltpu
from jax.sharding import Mesh, PartitionSpec as P

HI = lax.Precision.HIGHEST
BITS = 9
NAMES = tuple("b%d" % bit for bit in reversed(range(BITS)))
TOP = 5
ROUNDS = (9, 7, 6, 6, 5, 5, 5, 5, 5)
N = 128


def axes(low, high):
    return tuple("b%d" % bit for bit in reversed(range(low, high)))


def dot(a, b):
    return jnp.dot(a, b, precision=HI, preferred_element_type=jnp.float32)


def tdot(a, b):
    return lax.dot_general(a, b, (((0,), (0,)), ((), ())), precision=HI, preferred_element_type=jnp.float32)


def quick(a, b):
    return jnp.dot(a.astype(jnp.bfloat16), b.astype(jnp.bfloat16), preferred_element_type=jnp.float32)


def eye():
    row = lax.broadcasted_iota(jnp.int32, (N, N), 0)
    col = lax.broadcasted_iota(jnp.int32, (N, N), 1)
    return (row == col).astype(jnp.float32)


def wide(ref, first, last):
    return jnp.concatenate([ref[i] for i in range(first, last)], axis=1)


def invert(matrix, start, rounds, out_ref):
    one = eye()
    value = start
    for _ in range(rounds):
        value = value + quick(value, one - quick(matrix, value))
    for _ in range(2):
        rest = one - dot(matrix, value)
        value = value + quick(value, rest)
    out_ref[...] = value
    left = jnp.sum(rest * rest)

    @pl.when(jnp.logical_not(left < 1e-6))
    def _():
        out_ref[...] = jnp.where(left < 0.25, value, start)

        def more(state):
            step, left = state
            return jnp.logical_and(step < 60, jnp.logical_not(left < 1e-9))

        def body(state):
            step, _ = state
            now = out_ref[...]
            rest = eye() - dot(matrix, now)
            out_ref[...] = now + dot(now, rest)
            return step + 1, jnp.sum(rest * rest)

        lax.while_loop(more, body, (jnp.int32(0), jnp.float32(1.0)))


def general_start(matrix):
    size = jnp.abs(matrix)
    by_col = jnp.max(jnp.sum(size, axis=0, keepdims=True), axis=1, keepdims=True)
    by_row = jnp.max(jnp.sum(size, axis=1, keepdims=True), axis=0, keepdims=True)
    return matrix.T * (1.9 / (by_col * by_row))


def spread(ref, base, value):
    for i in range(value.shape[1] // N):
        ref[base + i] = value[:, i * N : (i + 1) * N]


def side(blocks):
    return jnp.concatenate(blocks, axis=1)


def leaf_kernel(diag_ref, left_ref, right_ref, source_ref, work_ref, first_ref, second_ref, inv_ref):
    levels = left_ref.shape[0]
    diag = diag_ref[...]
    bound = jnp.max(jnp.sum(jnp.abs(diag), axis=0, keepdims=True), axis=1, keepdims=True)
    invert(diag, eye() * (2.0 / (1.0 + bound)), 6, inv_ref)
    rhs = jnp.concatenate([left_ref[i] for i in range(levels)] + [source_ref[...]], axis=1)
    work = dot(inv_ref[...], rhs)
    spread(work_ref, 0, work)
    spread(first_ref, 0, tdot(right_ref[0], work))
    spread(second_ref, 0, tdot(right_ref[1], work))


def own_coef(level, own, other, inv_ref):
    matrix = eye() - dot(other[0], own[0])
    invert(matrix, general_start(matrix), ROUNDS[level], inv_ref)
    right = side(other[1:]) - dot(other[0], side(own[1:]))
    return dot(inv_ref[...], right)


def advance(work_ref, coef, right_ref, next_ref, panel_ref):
    count = work_ref.shape[0]
    later = wide(work_ref, 1, count) - dot(work_ref[0], coef)
    spread(next_ref, 0, later)
    for k in range(right_ref.shape[0]):
        spread(panel_ref, k * (count - 1), tdot(right_ref[k], later))


def pair_kernel(own_ref, other_ref, work_ref, coef_ref, other_coef_ref, next_ref, inv_ref):
    count = work_ref.shape[0]
    coef = own_coef(0, [own_ref[i] for i in range(count)], [other_ref[i] for i in range(count)], inv_ref)
    coef_ref[...] = coef
    other_coef_ref[...] = wide(own_ref, 1, count) - dot(own_ref[0], coef)
    spread(next_ref, 0, wide(work_ref, 1, count) - dot(work_ref[0], coef))


def merge_kernel(flag_ref, own_ref, other_ref, coef_ref, other_coef_ref, front_ref, part_ref):
    count = own_ref.shape[0]
    total = wide(own_ref, 1, count) + wide(other_ref, 1, count)
    total = total - dot(own_ref[0], coef_ref[...]) - dot(other_ref[0], other_coef_ref[...])
    for i in range(count - 1):
        front_ref[i * N : (i + 1) * N] = total[:, i * N : (i + 1) * N]
    rows = part_ref.shape[0]
    part_ref[...] = front_ref[pl.ds(pl.multiple_of(flag_ref[0] * rows, 8), rows)]


def join(flag, mine_ref, swapped_ref, full_ref):
    rows = mine_ref.shape[0]
    full_ref[pl.ds(pl.multiple_of(flag * rows, 8), rows)] = mine_ref[...]
    full_ref[pl.ds(pl.multiple_of((1 - flag) * rows, 8), rows)] = swapped_ref[...]
    return [full_ref[i * N : (i + 1) * N] for i in range(2 * rows // N)]


def quad_kernel(flag_ref, own_ref, mine_ref, swapped_ref, work_ref, right_ref, next_ref, panel_ref, inv_ref, full_ref):
    count = work_ref.shape[0]
    own = [own_ref[i * N : (i + 1) * N] for i in range(count)]
    other = join(flag_ref[0], mine_ref, swapped_ref, full_ref)
    advance(work_ref, own_coef(1, own, other, inv_ref), right_ref, next_ref, panel_ref)


def level_kernel(level, flag_ref, both_ref, work_ref, right_ref, next_ref, panel_ref, inv_ref):
    count = work_ref.shape[0]
    half = flag_ref[level]
    own = both_ref[:, half].reshape(count, N, N)
    other = both_ref[:, 1 - half].reshape(count, N, N)
    coef = own_coef(level, [own[i] for i in range(count)], [other[i] for i in range(count)], inv_ref)
    advance(work_ref, coef, right_ref, next_ref, panel_ref)


def front_step(level, own, other, coef_ref, inv_ref):
    count = 10 - level
    coef = own_coef(level, own[:count], other[:count], inv_ref)
    spread(coef_ref, 0, coef)
    other_coef = side(own[1:count]) - dot(own[0], coef)
    merged = []
    for base in range(count, len(own), count):
        total = side(own[base + 1 : base + count]) + side(other[base + 1 : base + count])
        merged.append(total - dot(own[base], coef) - dot(other[base], other_coef))
    return merged


def core_kernel(flag_ref, own_ref, other_ref, coef_ref, front_ref, part_ref, inv_ref):
    size = own_ref.shape[0]
    merged = front_step(5, [own_ref[i] for i in range(size)], [other_ref[i] for i in range(size)], coef_ref, inv_ref)
    at = 0
    for total in merged:
        for i in range(total.shape[1] // N):
            front_ref[at * N : (at + 1) * N] = total[:, i * N : (i + 1) * N]
            at += 1
    rows = part_ref.shape[0]
    part_ref[...] = front_ref[pl.ds(pl.multiple_of(flag_ref[5] * rows, 8), rows)]


def joined_kernel(flag_ref, own_ref, mine_ref, swapped_ref, coef_ref, front_ref, inv_ref, full_ref):
    own = [own_ref[i * N : (i + 1) * N] for i in range(own_ref.shape[0] // N)]
    other = join(flag_ref[5], mine_ref, swapped_ref, full_ref)
    for k, total in enumerate(front_step(6, own, other, coef_ref, inv_ref)):
        spread(front_ref, 3 * k, total)


def front_kernel(own_ref, other_ref, coef_ref, front_ref, inv_ref):
    size = own_ref.shape[0]
    for k, total in enumerate(front_step(7, [own_ref[i] for i in range(size)], [other_ref[i] for i in range(size)], coef_ref, inv_ref)):
        spread(front_ref, 2 * k, total)


def last_kernel(own_ref, other_ref, work_ref, out_ref, inv_ref):
    coef = own_coef(8, [own_ref[0], own_ref[1]], [other_ref[0], other_ref[1]], inv_ref)
    out_ref[...] = work_ref[1] - dot(work_ref[0], coef)


def apply_kernel(work_ref, coef_ref, next_ref):
    count = work_ref.shape[0]
    spread(next_ref, 0, wide(work_ref, 1, count) - dot(work_ref[0], wide(coef_ref, 0, count - 1)))


def blocks(count):
    return jax.ShapeDtypeStruct((count, N, N), jnp.float32)


def flat(rows, cols=N):
    return jax.ShapeDtypeStruct((rows, cols), jnp.float32)


def call(body, name, outs, *args, flags=None, full=0, inverse=True):
    scratch = [pltpu.VMEM((N, N), jnp.float32)] if inverse else []
    if full:
        scratch.append(pltpu.VMEM((full, N), jnp.float32))
    specs = [pl.BlockSpec(memory_space=pltpu.VMEM) for _ in args]
    if flags is not None:
        specs = [pl.BlockSpec(memory_space=pltpu.SMEM)] + specs
        args = (flags,) + args
    return pl.pallas_call(body, out_shape=outs, in_specs=specs, scratch_shapes=scratch, name=name)(*args)


def partner(value, bit):
    return lax.ppermute(value, "b%d" % bit, [(0, 1), (1, 0)])


def exchange(value, names):
    return lax.all_to_all(value, names, 0, 0)


def tie(*values):
    return lax.optimization_barrier(values)


def half_sums(panel, level):
    size = 2 ** (level + 1)
    rows = panel.shape[0] * N // size
    names = axes(0, level + 1)
    pieces = exchange(panel.reshape(size, rows, N), names)
    sums = pieces.reshape(2, size // 2, rows, N).sum(axis=1)
    return exchange(jnp.broadcast_to(sums[None], (size, 2, rows, N)), names)


def total(panel, level):
    count = panel.shape[0]
    size = 2**level
    rows = count * N // size
    names = axes(0, level)
    pieces = exchange(panel.reshape(size, rows, N), names)
    part = pieces.sum(axis=0)
    return exchange(jnp.broadcast_to(part[None], (size, rows, N)), names).reshape(count, N, N)


def per_device(diag_blocks, left_bases, right_bases, sources):
    levels = left_bases.shape[0]
    targets = levels + 1
    flags = jnp.stack([lax.axis_index("b%d" % bit) for bit in range(BITS)]).astype(jnp.int32)
    done = []

    work, first, second = call(leaf_kernel, "leaf", (blocks(10), blocks(10), blocks(10)), diag_blocks, left_bases, right_bases[:2], sources)
    first_other = partner(first, 0)
    second_other = partner(second, 0)
    done.append(work[0])
    coef, other_coef, work = call(pair_kernel, "pair", (flat(N, 9 * N), flat(N, 9 * N), blocks(9)), first, first_other, work)
    front, part = call(merge_kernel, "merge", (flat(9 * N), flat(9 * N // 2)), second, second_other, coef, other_coef, flags=flags, inverse=False)
    mine = partner(part, 1)
    swapped = partner(mine, 0)
    done.append(work[0])
    work, panel = call(quad_kernel, "quad", (blocks(8), blocks(8)), front, mine, swapped, work, right_bases[2:3], flags=flags, full=9 * N)

    for level in range(2, TOP):
        count = targets - level
        both = half_sums(panel, level)
        rows = 1 if level + 1 < TOP else levels - TOP

        def body(*refs, level=level):
            level_kernel(level, *refs)

        done.append(work[0])
        work, panel = call(
            body,
            "level%d" % level,
            (blocks(count - 1), blocks(rows * (count - 1))),
            both,
            work,
            right_bases[level + 1 : level + 1 + rows],
            flags=flags,
        )

    front = total(panel, TOP)
    other = partner(front, 5)
    done.append(work[0])
    coef, front, part = call(core_kernel, "front5", (blocks(4), flat(12 * N), flat(6 * N)), front, other, flags=flags)
    mine = partner(part, 6)
    work = call(apply_kernel, "apply5", blocks(4), work, coef, inverse=False)
    done.append(work[0])
    mine, work = tie(mine, work)
    swapped = partner(mine, 5)
    coef, front = call(joined_kernel, "front6", (blocks(3), blocks(6)), front, mine, swapped, flags=flags, full=12 * N)
    other = partner(front, 7)
    work = call(apply_kernel, "apply6", blocks(3), work, coef, inverse=False)
    done.append(work[0])
    other, work = tie(other, work)
    coef, front = call(front_kernel, "front7", (blocks(2), blocks(2)), front, other)
    other = partner(front, 8)
    work = call(apply_kernel, "apply7", blocks(2), work, coef, inverse=False)
    done.append(work[0])
    updated = jnp.stack(done)
    other, work, updated = tie(other, work, updated)
    out = call(last_kernel, "front8", flat(N), front, other, work)
    return updated, out


def solution(mesh):
    fine = Mesh(mesh.devices.reshape((2,) * BITS), NAMES)
    rows = P(NAMES, None)
    stacked = P(None, NAMES, None)
    return jax.shard_map(
        per_device,
        mesh=fine,
        in_specs=(rows, stacked, stacked, rows),
        out_specs=(stacked, rows),
        check_vma=False,
    )
```

```python
import jax
import jax.numpy as jnp
from jax import lax
from jax.experimental import pallas as pl
from jax.experimental.pallas import tpu as pltpu
from jax.sharding import Mesh, PartitionSpec as P

HI = lax.Precision.HIGHEST
BITS = 9
NAMES = tuple("b%d" % bit for bit in reversed(range(BITS)))
TOP = 5
ROUNDS = (9, 7, 6, 6, 5, 5, 5, 5, 5)
N = 128


def axes(low, high):
    return tuple("b%d" % bit for bit in reversed(range(low, high)))


def dot(a, b):
    return jnp.dot(a, b, precision=HI, preferred_element_type=jnp.float32)


def tdot(a, b):
    return lax.dot_general(a, b, (((0,), (0,)), ((), ())), precision=HI, preferred_element_type=jnp.float32)


def quick(a, b):
    return jnp.dot(a.astype(jnp.bfloat16), b.astype(jnp.bfloat16), preferred_element_type=jnp.float32)


def eye():
    row = lax.broadcasted_iota(jnp.int32, (N, N), 0)
    col = lax.broadcasted_iota(jnp.int32, (N, N), 1)
    return (row == col).astype(jnp.float32)


def wide(ref, first, last):
    return jnp.concatenate([ref[i] for i in range(first, last)], axis=1)


def invert(matrix, start, rounds, out_ref):
    one = eye()
    value = start
    for _ in range(rounds):
        value = value + quick(value, one - quick(matrix, value))
    for _ in range(2):
        rest = one - dot(matrix, value)
        value = value + quick(value, rest)
    out_ref[...] = value
    left = jnp.sum(rest * rest)

    @pl.when(jnp.logical_not(left < 1e-6))
    def _():
        out_ref[...] = jnp.where(left < 0.25, value, start)

        def more(state):
            step, left = state
            return jnp.logical_and(step < 60, jnp.logical_not(left < 1e-9))

        def body(state):
            step, _ = state
            now = out_ref[...]
            rest = eye() - dot(matrix, now)
            out_ref[...] = now + dot(now, rest)
            return step + 1, jnp.sum(rest * rest)

        lax.while_loop(more, body, (jnp.int32(0), jnp.float32(1.0)))


def general_start(matrix):
    size = jnp.abs(matrix)
    by_col = jnp.max(jnp.sum(size, axis=0, keepdims=True), axis=1, keepdims=True)
    by_row = jnp.max(jnp.sum(size, axis=1, keepdims=True), axis=0, keepdims=True)
    return matrix.T * (1.9 / (by_col * by_row))


def spread(ref, base, value):
    for i in range(value.shape[1] // N):
        ref[base + i] = value[:, i * N : (i + 1) * N]


def side(blocks):
    return jnp.concatenate(blocks, axis=1)


class Fetch:
    def __init__(self, source, low, cuts, buffer, sems):
        self.buffer = buffer
        self.copies = [
            pltpu.make_async_copy(source.at[pl.ds(low + at, end - at)], buffer.at[pl.ds(at, end - at)], sems.at[i])
            for i, (at, end) in enumerate(zip(cuts[:-1], cuts[1:]))
        ]
        self.waited = 0

    def need(self, pieces=None):
        pieces = len(self.copies) if pieces is None else pieces
        while self.waited < pieces:
            self.copies[self.waited].wait()
            self.waited += 1
        return self.buffer


def call(body, name, outs, *args, flags=None, full=0, inverse=True):
    arrays, lows, cuts = [], [], []
    for arg in args:
        array, low, cut = arg if isinstance(arg, tuple) else (arg, 0, (0, arg.shape[0]))
        arrays.append(array)
        lows.append(low)
        cuts.append(cut)
    count = len(arrays)
    scratch = [pltpu.VMEM((cut[-1],) + array.shape[1:], jnp.float32) for array, cut in zip(arrays, cuts)]
    scratch += [pltpu.SemaphoreType.DMA((len(cut) - 1,)) for cut in cuts]
    if inverse:
        scratch.append(pltpu.VMEM((N, N), jnp.float32))
    if full:
        scratch.append(pltpu.VMEM((full, N), jnp.float32))
    results = outs if isinstance(outs, tuple) else (outs,)

    def kernel(*refs):
        flag_ref = None
        if flags is not None:
            flag_ref, refs = refs[0], refs[1:]
        sources, refs = refs[:count], refs[count:]
        targets, refs = refs[: len(results)], refs[len(results) :]
        buffers, sems, extra = refs[:count], refs[count : 2 * count], refs[2 * count :]
        fetches = [Fetch(*one) for one in zip(sources, lows, cuts, buffers, sems)]
        for piece in range(max(len(cut) - 1 for cut in cuts)):
            for fetch in fetches:
                if piece < len(fetch.copies):
                    fetch.copies[piece].start()
        body(flag_ref, fetches, targets, *extra)
        for fetch in fetches:
            fetch.need()

    specs = [pl.BlockSpec(memory_space=pl.ANY) for _ in arrays]
    if flags is not None:
        specs = [pl.BlockSpec(memory_space=pltpu.SMEM)] + specs
        arrays = [flags] + arrays
    return pl.pallas_call(kernel, out_shape=outs, in_specs=specs, scratch_shapes=scratch, name=name)(*arrays)


def stacked_first(array):
    return (array, 0, (0, 1, array.shape[0]))


def flat_first(array):
    return (array, 0, (0, N, array.shape[0]))


def flat_wide(ref, first, last):
    return side([ref[i * N : (i + 1) * N] for i in range(first, last)])


def put_flat(ref, base, value):
    for i in range(value.shape[1] // N):
        ref[(base + i) * N : (base + i + 1) * N] = value[:, i * N : (i + 1) * N]


def leaf_body(flag_ref, fetches, outs, inv_ref):
    diag_f, left_f, source_f, right_f = fetches
    diag = diag_f.need()[...]
    bound = jnp.max(jnp.sum(jnp.abs(diag), axis=0, keepdims=True), axis=1, keepdims=True)
    start = eye() * (2.0 / (1.0 + bound))
    left = left_f.need()
    source = source_f.need()
    right = right_f.need()
    invert(diag, start, 6, inv_ref)
    rhs = jnp.concatenate([left[i] for i in range(left.shape[0])] + [source[...]], axis=1)
    work = dot(inv_ref[...], rhs)
    spread(outs[0], 0, work)
    for k in range(right.shape[0]):
        spread(outs[1 + k], 0, tdot(right[k], work))


def solve(level, own_g, other_g, rest, inv_ref):
    matrix = eye() - dot(other_g, own_g)
    start = general_start(matrix)
    own_p, other_p = rest()
    right = other_p - dot(other_g, own_p)
    invert(matrix, start, ROUNDS[level], inv_ref)
    return own_p, dot(inv_ref[...], right)


def pair_body(flag_ref, fetches, outs, inv_ref):
    own_f, other_f, work_f = fetches
    count = work_f.buffer.shape[0]
    own_g, other_g = own_f.need(1)[0], other_f.need(1)[0]

    def rest():
        own, other = wide(own_f.need(), 1, count), wide(other_f.need(), 1, count)
        work_f.need()
        return own, other

    own_p, coef = solve(0, own_g, other_g, rest, inv_ref)
    outs[0][...] = coef
    outs[1][...] = own_p - dot(own_g, coef)
    work = work_f.buffer
    spread(outs[2], 0, wide(work, 1, count) - dot(work[0], coef))


def merge_body(flag_ref, fetches, outs):
    coef_f, other_coef_f, own_f, other_f = fetches
    coef, other_coef, own, other = (fetch.need() for fetch in fetches)
    count = own.shape[0]
    merged = wide(own, 1, count) + wide(other, 1, count) - dot(own[0], coef[...]) - dot(other[0], other_coef[...])
    put_flat(outs[0], 0, merged)
    rows = outs[1].shape[0]
    outs[1][...] = outs[0][pl.ds(pl.multiple_of(flag_ref[0] * rows, 8), rows)]


def join(flag, mine_f, swapped_f, full_ref):
    rows = mine_f.buffer.shape[0]
    full_ref[pl.ds(pl.multiple_of(flag * rows, 8), rows)] = mine_f.need()[...]
    full_ref[pl.ds(pl.multiple_of((1 - flag) * rows, 8), rows)] = swapped_f.need()[...]
    return full_ref


def quad_body(flag_ref, fetches, outs, inv_ref, full_ref):
    own_f, mine_f, swapped_f, work_f = fetches
    count = work_f.buffer.shape[0]
    other = join(flag_ref[0], mine_f, swapped_f, full_ref)
    own = own_f.need()

    def rest():
        work_f.need()
        return flat_wide(own, 1, count), flat_wide(other, 1, count)

    own_p, coef = solve(1, own[:N], other[:N], rest, inv_ref)
    outs[0][...] = coef
    outs[1][...] = own_p - dot(own[:N], coef)
    work = work_f.buffer
    spread(outs[2], 0, wide(work, 1, count) - dot(work[0], coef))


def quad_merge_body(flag_ref, fetches, outs, full_ref):
    coef_f, other_coef_f, own_f, mine_f, swapped_f = fetches
    other = join(flag_ref[0], mine_f, swapped_f, full_ref)
    own, coef, other_coef = own_f.need(), coef_f.need(), other_coef_f.need()
    count = own.shape[0] // N
    merged = flat_wide(own, 1, count) + flat_wide(other, 1, count) - dot(own[:N], coef[...]) - dot(other[:N], other_coef[...])
    put_flat(outs[0], 0, merged)
    rows = outs[1].shape[0]
    outs[1][...] = outs[0][pl.ds(pl.multiple_of((2 * flag_ref[1] + flag_ref[0]) * rows, 8), rows)]


def finish(level, own_g, other_g, panels, work_f, right_f, outs, inv_ref):
    count = work_f.buffer.shape[0]
    before = []

    def rest():
        own_p, other_p = panels()
        work, right = work_f.need(), right_f.need()
        for k in range(right.shape[0]):
            before.append(tdot(right[k], wide(work, 0, count)))
        return own_p, other_p

    _, coef = solve(level, own_g, other_g, rest, inv_ref)
    for k, product in enumerate(before):
        spread(outs[1], k * (count - 1), product[:, N:] - dot(product[:, :N], coef))
    work = work_f.buffer
    spread(outs[0], 0, wide(work, 1, count) - dot(work[0], coef))


def octet_body(flag_ref, fetches, outs, inv_ref):
    own_f, other_f, work_f, right_f = fetches
    count = work_f.buffer.shape[0]
    own_g, other_g = own_f.need(1)[:N], other_f.need(1)[:N]

    def panels():
        return flat_wide(own_f.need(), 1, count), flat_wide(other_f.need(), 1, count)

    finish(2, own_g, other_g, panels, work_f, right_f, outs, inv_ref)


def level_body(level, flag_ref, fetches, outs, inv_ref):
    both_f, work_f, right_f = fetches
    count = work_f.buffer.shape[0]
    half = flag_ref[level]
    rows = both_f.buffer.shape[2]
    lead = -(-N // rows)
    first = both_f.need(1)
    own_g = first[:lead, half].reshape(lead * rows, N)[:N]
    other_g = first[:lead, 1 - half].reshape(lead * rows, N)[:N]

    def panels():
        both = both_f.need()
        return tuple(
            side([value[i] for i in range(1, count)])
            for value in (both[:, half].reshape(count, N, N), both[:, 1 - half].reshape(count, N, N))
        )

    finish(level, own_g, other_g, panels, work_f, right_f, outs, inv_ref)


def front_step(level, own_g, other_g, own, other, coef_ref, inv_ref):
    count = 10 - level
    readers = []

    def rest():
        readers.extend([own(), other()])
        return tuple(side([read(i) for i in range(1, count)]) for read in readers)

    own_p, coef = solve(level, own_g, other_g, rest, inv_ref)
    spread(coef_ref, 0, coef)
    other_coef = own_p - dot(own_g, coef)
    mine, yours = readers
    for base in range(count, count * (count - 1), count):
        both = side([mine(base + i) + yours(base + i) for i in range(1, count)])
        yield both - dot(mine(base), coef) - dot(yours(base), other_coef)


def stacked_reader(fetch):
    ref = fetch.need()
    return lambda i: ref[i]


def core_body(flag_ref, fetches, outs, inv_ref):
    own_f, other_f = fetches
    own_g, other_g = own_f.need(1)[0], other_f.need(1)[0]
    readers = [lambda fetch=fetch: stacked_reader(fetch) for fetch in fetches]
    for k, merged in enumerate(front_step(5, own_g, other_g, *readers, outs[0], inv_ref)):
        put_flat(outs[1], 4 * k, merged)
    rows = outs[2].shape[0]
    outs[2][...] = outs[1][pl.ds(pl.multiple_of(flag_ref[5] * rows, 8), rows)]


def joined_body(flag_ref, fetches, outs, inv_ref, full_ref):
    own_f, mine_f, swapped_f = fetches
    other = join(flag_ref[5], mine_f, swapped_f, full_ref)
    own = own_f.need()
    readers = [lambda ref=ref: (lambda i: ref[i * N : (i + 1) * N]) for ref in (own, other)]
    for k, merged in enumerate(front_step(6, own[:N], other[:N], *readers, outs[0], inv_ref)):
        spread(outs[1], 3 * k, merged)


def front_body(flag_ref, fetches, outs, inv_ref):
    own_f, other_f = fetches
    own_g, other_g = own_f.need(1)[0], other_f.need(1)[0]
    readers = [lambda fetch=fetch: stacked_reader(fetch) for fetch in fetches]
    for k, merged in enumerate(front_step(7, own_g, other_g, *readers, outs[0], inv_ref)):
        spread(outs[1], 2 * k, merged)


def last_body(flag_ref, fetches, outs, inv_ref):
    own_f, other_f, work_f = fetches
    own_g, other_g = own_f.need()[0], other_f.need()[0]

    def rest():
        work_f.need()
        return own_f.buffer[1], other_f.buffer[1]

    _, coef = solve(8, own_g, other_g, rest, inv_ref)
    outs[0][...] = work_f.buffer[1] - dot(work_f.buffer[0], coef)


def apply_body(flag_ref, fetches, outs):
    work, coef = (fetch.need() for fetch in fetches)
    count = work.shape[0]
    spread(outs[0], 0, wide(work, 1, count) - dot(work[0], wide(coef, 0, count - 1)))


def blocks(count):
    return jax.ShapeDtypeStruct((count, N, N), jnp.float32)


def flat(rows, cols=N):
    return jax.ShapeDtypeStruct((rows, cols), jnp.float32)


def partner(value, bit):
    return lax.ppermute(value, "b%d" % bit, [(0, 1), (1, 0)])


def exchange(value, names):
    return lax.all_to_all(value, names, 0, 0)


def tie(*values):
    return lax.optimization_barrier(values)


def half_sums(panel, level):
    size = 2 ** (level + 1)
    rows = panel.shape[0] * N // size
    names = axes(0, level + 1)
    pieces = exchange(panel.reshape(size, rows, N), names)
    sums = pieces.reshape(2, size // 2, rows, N).sum(axis=1)
    return exchange(jnp.broadcast_to(sums[None], (size, 2, rows, N)), names)


def total(panel, level):
    count = panel.shape[0]
    size = 2**level
    rows = count * N // size
    names = axes(0, level)
    pieces = exchange(panel.reshape(size, rows, N), names)
    part = pieces.sum(axis=0)
    return exchange(jnp.broadcast_to(part[None], (size, rows, N)), names).reshape(count, N, N)


def per_device(diag_blocks, left_bases, right_bases, sources):
    levels = left_bases.shape[0]
    targets = levels + 1
    flags = jnp.stack([lax.axis_index("b%d" % bit) for bit in range(BITS)]).astype(jnp.int32)
    done = []

    def some_right(low, high):
        return (right_bases, low, (0, high - low))

    work, *panels = call(
        leaf_body, "leaf", (blocks(10), blocks(10), blocks(10), blocks(10)), diag_blocks, left_bases, sources, some_right(0, 3)
    )
    others = [partner(panel, 0) for panel in panels]
    done.append(work[0])
    coef, other_coef, work = call(
        pair_body, "pair", (flat(N, 9 * N), flat(N, 9 * N), blocks(9)), stacked_first(panels[0]), stacked_first(others[0]), work
    )
    done.append(work[0])
    fronts, mine = [], []
    for k in (1, 2):
        front, part = call(
            merge_body, "merge%d" % k, (flat(9 * N), flat(9 * N // 2)), coef, other_coef, panels[k], others[k], flags=flags, inverse=False
        )
        fronts.append(front)
        mine.append(partner(part, 1))
    swapped = [partner(part, 0) for part in mine]
    coef, other_coef, work = call(
        quad_body, "quad", (flat(N, 8 * N), flat(N, 8 * N), blocks(8)), fronts[0], mine[0], swapped[0], work, flags=flags, full=9 * N
    )
    done.append(work[0])
    front, part = call(
        quad_merge_body,
        "quadmerge",
        (flat(8 * N), flat(2 * N)),
        coef,
        other_coef,
        fronts[1],
        mine[1],
        swapped[1],
        flags=flags,
        full=9 * N,
        inverse=False,
    )
    part = partner(part, 2)
    other = exchange(jnp.broadcast_to(part[None], (4, 2 * N, N)), axes(0, 2)).reshape(8 * N, N)
    work, panel = call(
        octet_body, "octet", (blocks(7), blocks(7)), flat_first(front), flat_first(other), work, some_right(3, 4)
    )
    done.append(work[0])

    for level in range(3, TOP):
        count = targets - level
        both = half_sums(panel, level)
        size, _, piece, _ = both.shape
        rows = 1 if level + 1 < TOP else levels - TOP

        def body(*refs, level=level):
            level_body(level, *refs)

        work, panel = call(
            body,
            "level%d" % level,
            (blocks(count - 1), blocks(rows * (count - 1))),
            (both, 0, (0, -(-N // piece), size)),
            work,
            some_right(level + 1, level + 1 + rows),
            flags=flags,
        )
        done.append(work[0])

    front = total(panel, TOP)
    other = partner(front, 5)
    coef, front, part = call(
        core_body, "front5", (blocks(4), flat(12 * N), flat(6 * N)), stacked_first(front), stacked_first(other), flags=flags
    )
    mine = partner(part, 6)
    work = call(apply_body, "apply5", blocks(4), work, coef, inverse=False)
    done.append(work[0])
    mine, work = tie(mine, work)
    swapped = partner(mine, 5)
    coef, front = call(joined_body, "front6", (blocks(3), blocks(6)), front, mine, swapped, flags=flags, full=12 * N)
    other = partner(front, 7)
    work = call(apply_body, "apply6", blocks(3), work, coef, inverse=False)
    done.append(work[0])
    other, work = tie(other, work)
    coef, front = call(front_body, "front7", (blocks(2), blocks(2)), stacked_first(front), stacked_first(other))
    other = partner(front, 8)
    work = call(apply_body, "apply7", blocks(2), work, coef, inverse=False)
    done.append(work[0])
    updated = jnp.stack(done)
    other, work, updated = tie(other, work, updated)
    out = call(last_body, "front8", flat(N), front, other, work)
    return updated, out


def solution(mesh):
    fine = Mesh(mesh.devices.reshape((2,) * BITS), NAMES)
    rows = P(NAMES, None)
    stacked = P(None, NAMES, None)
    return jax.shard_map(
        per_device,
        mesh=fine,
        in_specs=(rows, stacked, stacked, rows),
        out_specs=(stacked, rows),
        check_vma=False,
    )
```

```python
import jax
import jax.numpy as jnp
from jax import lax
from jax.experimental import pallas as pl
from jax.experimental.pallas import tpu as pltpu
from jax.sharding import Mesh, PartitionSpec as P

HI = lax.Precision.HIGHEST
BITS = 9
NAMES = tuple("b%d" % bit for bit in reversed(range(BITS)))
TOP = 5
ROUNDS = (9, 7, 6, 6, 5, 5, 5, 5, 5)
N = 128


def axes(low, high):
    return tuple("b%d" % bit for bit in reversed(range(low, high)))


def exact(a, b):
    return jnp.dot(a, b, precision=HI, preferred_element_type=jnp.float32)


def parts(value):
    high = value.astype(jnp.bfloat16)
    return high, (value - high.astype(jnp.float32)).astype(jnp.bfloat16)


def dot(a, b):
    a_high, a_low = parts(a)
    b_high, b_low = parts(b)

    def one(x, y):
        return jnp.dot(x, y, preferred_element_type=jnp.float32)

    return one(a_high, b_high) + (one(a_high, b_low) + one(a_low, b_high))


def tdot(a, b):
    return dot(a.T, b)


def quick(a, b):
    return jnp.dot(a.astype(jnp.bfloat16), b.astype(jnp.bfloat16), preferred_element_type=jnp.float32)


def eye():
    row = lax.broadcasted_iota(jnp.int32, (N, N), 0)
    col = lax.broadcasted_iota(jnp.int32, (N, N), 1)
    return (row == col).astype(jnp.float32)


def wide(ref, first, last):
    return jnp.concatenate([ref[i] for i in range(first, last)], axis=1)


def invert(matrix, start, rounds, out_ref):
    one = eye()
    value = start
    for _ in range(rounds):
        value = value + quick(value, one - quick(matrix, value))
    for product in (dot, exact):
        rest = one - product(matrix, value)
        value = value + quick(value, rest)
    out_ref[...] = value
    left = jnp.sum(rest * rest)

    @pl.when(jnp.logical_not(left < 1e-6))
    def _():
        out_ref[...] = jnp.where(left < 0.25, value, start)

        def more(state):
            step, left = state
            return jnp.logical_and(step < 60, jnp.logical_not(left < 1e-9))

        def body(state):
            step, _ = state
            now = out_ref[...]
            rest = eye() - exact(matrix, now)
            out_ref[...] = now + exact(now, rest)
            return step + 1, jnp.sum(rest * rest)

        lax.while_loop(more, body, (jnp.int32(0), jnp.float32(1.0)))


def general_start(matrix):
    size = jnp.abs(matrix)
    by_col = jnp.max(jnp.sum(size, axis=0, keepdims=True), axis=1, keepdims=True)
    by_row = jnp.max(jnp.sum(size, axis=1, keepdims=True), axis=0, keepdims=True)
    return matrix.T * (1.9 / (by_col * by_row))


def spread(ref, base, value):
    for i in range(value.shape[1] // N):
        ref[base + i] = value[:, i * N : (i + 1) * N]


def side(blocks):
    return jnp.concatenate(blocks, axis=1)


class Operand:
    def __init__(self, ref):
        self.buffer = ref

    def need(self, pieces=None):
        return self.buffer


def call(body, name, outs, *args, flags=None, full=0, inverse=True):
    arrays = [pltpu.with_memory_space_constraint(arg[0] if isinstance(arg, tuple) else arg, pltpu.VMEM) for arg in args]
    count = len(arrays)
    scratch = []
    if inverse:
        scratch.append(pltpu.VMEM((N, N), jnp.float32))
    if full:
        scratch.append(pltpu.VMEM((full, N), jnp.float32))
    results = outs if isinstance(outs, tuple) else (outs,)

    def kernel(*refs):
        flag_ref = None
        if flags is not None:
            flag_ref, refs = refs[0], refs[1:]
        operands = []
        for arg, ref in zip(args, refs[:count]):
            if isinstance(arg, tuple):
                ref = ref.at[pl.ds(arg[1], arg[2][-1])]
            operands.append(Operand(ref))
        refs = refs[count:]
        body(flag_ref, operands, refs[: len(results)], *refs[len(results) :])

    specs = [pl.BlockSpec(memory_space=pltpu.VMEM) for _ in arrays]
    if flags is not None:
        specs = [pl.BlockSpec(memory_space=pltpu.SMEM)] + specs
        arrays = [flags] + arrays
    params = pltpu.CompilerParams(vmem_limit_bytes=16 << 20)
    return pl.pallas_call(
        kernel, out_shape=outs, in_specs=specs, scratch_shapes=scratch, compiler_params=params, name=name
    )(*arrays)


def stacked_first(array):
    return (array, 0, (0, 1, array.shape[0]))


def flat_first(array):
    return (array, 0, (0, N, array.shape[0]))


def flat_wide(ref, first, last):
    return side([ref[i * N : (i + 1) * N] for i in range(first, last)])


def put_flat(ref, base, value):
    for i in range(value.shape[1] // N):
        ref[(base + i) * N : (base + i + 1) * N] = value[:, i * N : (i + 1) * N]


def leaf_body(flag_ref, fetches, outs, inv_ref):
    diag_f, left_f, source_f, right_f = fetches
    diag = diag_f.need()[...]
    bound = jnp.max(jnp.sum(jnp.abs(diag), axis=0, keepdims=True), axis=1, keepdims=True)
    start = eye() * (2.0 / (1.0 + bound))
    left = left_f.need()
    source = source_f.need()
    right = right_f.need()
    invert(diag, start, 6, inv_ref)
    rhs = jnp.concatenate([left[i] for i in range(left.shape[0])] + [source[...]], axis=1)
    work = dot(inv_ref[...], rhs)
    spread(outs[0], 0, work)
    for k in range(right.shape[0]):
        spread(outs[1 + k], 0, tdot(right[k], work))


def solve(level, own_g, other_g, rest, inv_ref):
    matrix = eye() - dot(other_g, own_g)
    start = general_start(matrix)
    own_p, other_p = rest()
    right = other_p - dot(other_g, own_p)
    invert(matrix, start, ROUNDS[level], inv_ref)
    return own_p, dot(inv_ref[...], right)


def pair_body(flag_ref, fetches, outs, inv_ref):
    own_f, other_f, work_f = fetches
    count = work_f.buffer.shape[0]
    own_g, other_g = own_f.need(1)[0], other_f.need(1)[0]

    def rest():
        own, other = wide(own_f.need(), 1, count), wide(other_f.need(), 1, count)
        work_f.need()
        return own, other

    own_p, coef = solve(0, own_g, other_g, rest, inv_ref)
    outs[0][...] = coef
    outs[1][...] = own_p - dot(own_g, coef)
    work = work_f.buffer
    spread(outs[2], 0, wide(work, 1, count) - dot(work[0], coef))


def merge_body(flag_ref, fetches, outs):
    coef_f, other_coef_f, own_f, other_f = fetches
    coef, other_coef, own, other = (fetch.need() for fetch in fetches)
    count = own.shape[0]
    merged = wide(own, 1, count) + wide(other, 1, count) - dot(own[0], coef[...]) - dot(other[0], other_coef[...])
    put_flat(outs[0], 0, merged)
    rows = outs[1].shape[0]
    outs[1][...] = outs[0][pl.ds(pl.multiple_of(flag_ref[0] * rows, 8), rows)]


def join(flag, mine_f, swapped_f, full_ref):
    rows = mine_f.buffer.shape[0]
    full_ref[pl.ds(pl.multiple_of(flag * rows, 8), rows)] = mine_f.need()[...]
    full_ref[pl.ds(pl.multiple_of((1 - flag) * rows, 8), rows)] = swapped_f.need()[...]
    return full_ref


def quad_body(flag_ref, fetches, outs, inv_ref, full_ref):
    own_f, mine_f, swapped_f, work_f = fetches
    count = work_f.buffer.shape[0]
    other = join(flag_ref[0], mine_f, swapped_f, full_ref)
    own = own_f.need()

    def rest():
        work_f.need()
        return flat_wide(own, 1, count), flat_wide(other, 1, count)

    own_p, coef = solve(1, own[:N], other[:N], rest, inv_ref)
    outs[0][...] = coef
    outs[1][...] = own_p - dot(own[:N], coef)
    work = work_f.buffer
    spread(outs[2], 0, wide(work, 1, count) - dot(work[0], coef))


def quad_merge_body(flag_ref, fetches, outs, full_ref):
    coef_f, other_coef_f, own_f, mine_f, swapped_f = fetches
    other = join(flag_ref[0], mine_f, swapped_f, full_ref)
    own, coef, other_coef = own_f.need(), coef_f.need(), other_coef_f.need()
    count = own.shape[0] // N
    merged = flat_wide(own, 1, count) + flat_wide(other, 1, count) - dot(own[:N], coef[...]) - dot(other[:N], other_coef[...])
    put_flat(outs[0], 0, merged)
    rows = outs[1].shape[0]
    outs[1][...] = outs[0][pl.ds(pl.multiple_of((2 * flag_ref[1] + flag_ref[0]) * rows, 8), rows)]


def finish(level, own_g, other_g, panels, work_f, right_f, outs, inv_ref):
    work, right = work_f.need(), right_f.need()
    count = work.shape[0]
    _, coef = solve(level, own_g, other_g, panels, inv_ref)
    later = wide(work, 1, count) - dot(work[0], coef)
    for k in range(right.shape[0]):
        spread(outs[1], k * (count - 1), tdot(right[k], later))
    spread(outs[0], 0, later)


def octet_body(flag_ref, fetches, outs, inv_ref):
    own_f, other_f, work_f, right_f = fetches
    count = work_f.buffer.shape[0]
    own_g, other_g = own_f.need(1)[:N], other_f.need(1)[:N]

    def panels():
        return flat_wide(own_f.need(), 1, count), flat_wide(other_f.need(), 1, count)

    finish(2, own_g, other_g, panels, work_f, right_f, outs, inv_ref)


def level_body(level, flag_ref, fetches, outs, inv_ref):
    both_f, work_f, right_f = fetches
    count = work_f.buffer.shape[0]
    half = flag_ref[level]
    rows = both_f.buffer.shape[2]
    lead = -(-N // rows)
    first = both_f.need(1)
    own_g = first[:lead, half].reshape(lead * rows, N)[:N]
    other_g = first[:lead, 1 - half].reshape(lead * rows, N)[:N]

    def panels():
        both = both_f.need()
        return tuple(
            side([value[i] for i in range(1, count)])
            for value in (both[:, half].reshape(count, N, N), both[:, 1 - half].reshape(count, N, N))
        )

    finish(level, own_g, other_g, panels, work_f, right_f, outs, inv_ref)


def front_step(level, own_g, other_g, own, other, coef_ref, inv_ref):
    count = 10 - level
    readers = []

    def rest():
        readers.extend([own(), other()])
        return tuple(side([read(i) for i in range(1, count)]) for read in readers)

    own_p, coef = solve(level, own_g, other_g, rest, inv_ref)
    spread(coef_ref, 0, coef)
    other_coef = own_p - dot(own_g, coef)
    mine, yours = readers
    for base in range(count, count * (count - 1), count):
        both = side([mine(base + i) + yours(base + i) for i in range(1, count)])
        yield both - dot(mine(base), coef) - dot(yours(base), other_coef)


def stacked_reader(fetch):
    ref = fetch.need()
    return lambda i: ref[i]


def core_body(flag_ref, fetches, outs, inv_ref):
    own_f, other_f = fetches
    own_g, other_g = own_f.need(1)[0], other_f.need(1)[0]
    readers = [lambda fetch=fetch: stacked_reader(fetch) for fetch in fetches]
    for k, merged in enumerate(front_step(5, own_g, other_g, *readers, outs[0], inv_ref)):
        put_flat(outs[1], 4 * k, merged)
    rows = outs[2].shape[0]
    outs[2][...] = outs[1][pl.ds(pl.multiple_of(flag_ref[5] * rows, 8), rows)]


def joined_body(flag_ref, fetches, outs, inv_ref, full_ref):
    own_f, mine_f, swapped_f = fetches
    other = join(flag_ref[5], mine_f, swapped_f, full_ref)
    own = own_f.need()
    readers = [lambda ref=ref: (lambda i: ref[i * N : (i + 1) * N]) for ref in (own, other)]
    for k, merged in enumerate(front_step(6, own[:N], other[:N], *readers, outs[0], inv_ref)):
        spread(outs[1], 3 * k, merged)


def front_body(flag_ref, fetches, outs, inv_ref):
    own_f, other_f = fetches
    own_g, other_g = own_f.need(1)[0], other_f.need(1)[0]
    readers = [lambda fetch=fetch: stacked_reader(fetch) for fetch in fetches]
    for k, merged in enumerate(front_step(7, own_g, other_g, *readers, outs[0], inv_ref)):
        spread(outs[1], 2 * k, merged)


def last_body(flag_ref, fetches, outs, inv_ref):
    own_f, other_f, work_f = fetches
    own_g, other_g = own_f.need()[0], other_f.need()[0]

    def rest():
        work_f.need()
        return own_f.buffer[1], other_f.buffer[1]

    _, coef = solve(8, own_g, other_g, rest, inv_ref)
    outs[0][...] = work_f.buffer[1] - dot(work_f.buffer[0], coef)


def apply_body(flag_ref, fetches, outs):
    work, coef = (fetch.need() for fetch in fetches)
    count = work.shape[0]
    spread(outs[0], 0, wide(work, 1, count) - dot(work[0], wide(coef, 0, count - 1)))


def blocks(count):
    return pltpu.VMEM((count, N, N), jnp.float32)


def flat(rows, cols=N):
    return pltpu.VMEM((rows, cols), jnp.float32)


def partner(value, bit):
    return lax.ppermute(value, "b%d" % bit, [(0, 1), (1, 0)])


def exchange(value, names):
    return lax.all_to_all(value, names, 0, 0)


def tie(*values):
    return lax.optimization_barrier(values)


def half_sums(panel, level):
    size = 2 ** (level + 1)
    rows = panel.shape[0] * N // size
    names = axes(0, level + 1)
    pieces = exchange(panel.reshape(size, rows, N), names)
    sums = pieces.reshape(2, size // 2, rows, N).sum(axis=1)
    return exchange(jnp.broadcast_to(sums[None], (size, 2, rows, N)), names)


def total(panel, level):
    count = panel.shape[0]
    size = 2**level
    rows = count * N // size
    names = axes(0, level)
    pieces = exchange(panel.reshape(size, rows, N), names)
    part = pieces.sum(axis=0)
    return exchange(jnp.broadcast_to(part[None], (size, rows, N)), names).reshape(count, N, N)


def per_device(diag_blocks, left_bases, right_bases, sources):
    levels = left_bases.shape[0]
    targets = levels + 1
    flags = jnp.stack([lax.axis_index("b%d" % bit) for bit in range(BITS)]).astype(jnp.int32)
    done = []

    def some_right(low, high):
        return (right_bases, low, (0, high - low))

    work, *panels = call(
        leaf_body, "leaf", (blocks(10), blocks(10), blocks(10), blocks(10)), diag_blocks, left_bases, sources, some_right(0, 3)
    )
    others = [partner(panels[0], 0)]
    panels[1], others[0] = tie(panels[1], others[0])
    others.append(partner(panels[1], 0))
    done.append(work[0])
    coef, other_coef, work = call(
        pair_body, "pair", (flat(N, 9 * N), flat(N, 9 * N), blocks(9)), stacked_first(panels[0]), stacked_first(others[0]), work
    )
    done.append(work[0])
    panels[2], others[1], coef = tie(panels[2], others[1], coef)
    others.append(partner(panels[2], 0))
    fronts, mine = [], []
    for k in (1, 2):
        front, part = call(
            merge_body, "merge%d" % k, (flat(9 * N), flat(9 * N // 2)), coef, other_coef, panels[k], others[k], flags=flags, inverse=False
        )
        fronts.append(front)
        mine.append(partner(part, 1))
    swapped = [partner(mine[0], 0)]
    coef, other_coef, work = call(
        quad_body, "quad", (flat(N, 8 * N), flat(N, 8 * N), blocks(8)), fronts[0], mine[0], swapped[0], work, flags=flags, full=9 * N
    )
    coef, mine[1] = tie(coef, mine[1])
    swapped.append(partner(mine[1], 0))
    done.append(work[0])
    front, part = call(
        quad_merge_body,
        "quadmerge",
        (flat(8 * N), flat(2 * N)),
        coef,
        other_coef,
        fronts[1],
        mine[1],
        swapped[1],
        flags=flags,
        full=9 * N,
        inverse=False,
    )
    part = partner(part, 2)
    other = exchange(jnp.broadcast_to(part[None], (4, 2 * N, N)), axes(0, 2)).reshape(8 * N, N)
    work, panel = call(
        octet_body, "octet", (blocks(7), blocks(7)), flat_first(front), flat_first(other), work, some_right(3, 4)
    )
    done.append(work[0])

    for level in range(3, TOP):
        count = targets - level
        both = half_sums(panel, level)
        size, _, piece, _ = both.shape
        rows = 1 if level + 1 < TOP else levels - TOP

        def body(*refs, level=level):
            level_body(level, *refs)

        work, panel = call(
            body,
            "level%d" % level,
            (blocks(count - 1), blocks(rows * (count - 1))),
            (both, 0, (0, -(-N // piece), size)),
            work,
            some_right(level + 1, level + 1 + rows),
            flags=flags,
        )
        done.append(work[0])

    front = total(panel, TOP)
    other = partner(front, 5)
    coef, front, part = call(
        core_body, "front5", (blocks(4), flat(12 * N), flat(6 * N)), stacked_first(front), stacked_first(other), flags=flags
    )
    mine = partner(part, 6)
    work = call(apply_body, "apply5", blocks(4), work, coef, inverse=False)
    done.append(work[0])
    mine, work = tie(mine, work)
    swapped = partner(mine, 5)
    coef, front = call(joined_body, "front6", (blocks(3), blocks(6)), front, mine, swapped, flags=flags, full=12 * N)
    other = partner(front, 7)
    work = call(apply_body, "apply6", blocks(3), work, coef, inverse=False)
    done.append(work[0])
    other, work = tie(other, work)
    coef, front = call(front_body, "front7", (blocks(2), blocks(2)), stacked_first(front), stacked_first(other))
    other = partner(front, 8)
    work = call(apply_body, "apply7", blocks(2), work, coef, inverse=False)
    done.append(work[0])
    updated = jnp.stack(done)
    other, work, updated = tie(other, work, updated)
    out = call(last_body, "front8", flat(N), front, other, work)
    return updated, out


def solution(mesh):
    fine = Mesh(mesh.devices.reshape((2,) * BITS), NAMES)
    rows = P(NAMES, None)
    stacked = P(None, NAMES, None)
    return jax.shard_map(
        per_device,
        mesh=fine,
        in_specs=(rows, stacked, stacked, rows),
        out_specs=(stacked, rows),
        check_vma=False,
    )
```

```python
import jax
import jax.numpy as jnp
from jax import lax
from jax.experimental import pallas as pl
from jax.experimental.pallas import tpu as pltpu
from jax.sharding import Mesh, PartitionSpec as P

HI = lax.Precision.HIGHEST
BITS = 9
NAMES = tuple("b%d" % bit for bit in reversed(range(BITS)))
TOP = 5
ROUNDS = (9, 7, 6, 6, 5, 5, 5, 5, 5)
N = 128


def axes(low, high):
    return tuple("b%d" % bit for bit in reversed(range(low, high)))


def exact(a, b):
    return jnp.dot(a, b, precision=HI, preferred_element_type=jnp.float32)


def parts(value):
    high = value.astype(jnp.bfloat16)
    return high, (value - high.astype(jnp.float32)).astype(jnp.bfloat16)


def dot(a, b):
    a_high, a_low = parts(a)
    b_high, b_low = parts(b)

    def one(x, y):
        return jnp.dot(x, y, preferred_element_type=jnp.float32)

    return one(a_high, b_high) + (one(a_high, b_low) + one(a_low, b_high))


def tdot(a, b):
    return dot(a.T, b)


def quick(a, b):
    return jnp.dot(a.astype(jnp.bfloat16), b.astype(jnp.bfloat16), preferred_element_type=jnp.float32)


def eye():
    row = lax.broadcasted_iota(jnp.int32, (N, N), 0)
    col = lax.broadcasted_iota(jnp.int32, (N, N), 1)
    return (row == col).astype(jnp.float32)


def wide(ref, first, last):
    return jnp.concatenate([ref[i] for i in range(first, last)], axis=1)


def invert(matrix, start, rounds, out_ref):
    one = eye()
    value = start
    for _ in range(rounds):
        value = value + quick(value, one - quick(matrix, value))
    for product in (dot, exact):
        rest = one - product(matrix, value)
        value = value + quick(value, rest)
    out_ref[...] = value
    left = jnp.sum(rest * rest)

    @pl.when(jnp.logical_not(left < 1e-6))
    def _():
        out_ref[...] = jnp.where(left < 0.25, value, start)

        def more(state):
            step, left = state
            return jnp.logical_and(step < 60, jnp.logical_not(left < 1e-9))

        def body(state):
            step, _ = state
            now = out_ref[...]
            rest = eye() - exact(matrix, now)
            out_ref[...] = now + exact(now, rest)
            return step + 1, jnp.sum(rest * rest)

        lax.while_loop(more, body, (jnp.int32(0), jnp.float32(1.0)))


def general_start(matrix):
    size = jnp.abs(matrix)
    by_col = jnp.max(jnp.sum(size, axis=0, keepdims=True), axis=1, keepdims=True)
    by_row = jnp.max(jnp.sum(size, axis=1, keepdims=True), axis=0, keepdims=True)
    return matrix.T * (1.9 / (by_col * by_row))


def spread(ref, base, value):
    for i in range(value.shape[1] // N):
        ref[base + i] = value[:, i * N : (i + 1) * N]


def side(blocks):
    return jnp.concatenate(blocks, axis=1)


class Operand:
    def __init__(self, ref):
        self.buffer = ref

    def need(self, pieces=None):
        return self.buffer


def call(body, name, outs, *args, flags=None, full=0, inverse=True):
    arrays = [pltpu.with_memory_space_constraint(arg[0] if isinstance(arg, tuple) else arg, pltpu.VMEM) for arg in args]
    count = len(arrays)
    scratch = []
    if inverse:
        scratch.append(pltpu.VMEM((N, N), jnp.float32))
    if full:
        scratch.append(pltpu.VMEM((full, N), jnp.float32))
    results = outs if isinstance(outs, tuple) else (outs,)

    def kernel(*refs):
        flag_ref = None
        if flags is not None:
            flag_ref, refs = refs[0], refs[1:]
        operands = []
        for arg, ref in zip(args, refs[:count]):
            if isinstance(arg, tuple):
                ref = ref.at[pl.ds(arg[1], arg[2][-1])]
            operands.append(Operand(ref))
        refs = refs[count:]
        body(flag_ref, operands, refs[: len(results)], *refs[len(results) :])

    specs = [pl.BlockSpec(memory_space=pltpu.VMEM) for _ in arrays]
    if flags is not None:
        specs = [pl.BlockSpec(memory_space=pltpu.SMEM)] + specs
        arrays = [flags] + arrays
    params = pltpu.CompilerParams(vmem_limit_bytes=16 << 20)
    return pl.pallas_call(
        kernel, out_shape=outs, in_specs=specs, scratch_shapes=scratch, compiler_params=params, name=name
    )(*arrays)


def stacked_first(array):
    return (array, 0, (0, 1, array.shape[0]))


def flat_wide(ref, first, last):
    return side([ref[i * N : (i + 1) * N] for i in range(first, last)])


def put_flat(ref, base, value):
    for i in range(value.shape[1] // N):
        ref[(base + i) * N : (base + i + 1) * N] = value[:, i * N : (i + 1) * N]


def leaf_kernel(diag_any, left_any, source_any, right_any, work_ref, first_ref, second_ref, diag, left, source, right, sems, inv_ref):
    rows = right.shape[0]
    pairs = ((diag_any, diag), (left_any, left), (source_any, source), (right_any.at[pl.ds(0, rows)], right))
    copies = [pltpu.make_async_copy(*pair, sems.at[i]) for i, pair in enumerate(pairs)]
    for copy in copies:
        copy.start()
    copies[0].wait()
    block = diag[...]
    bound = jnp.max(jnp.sum(jnp.abs(block), axis=0, keepdims=True), axis=1, keepdims=True)
    invert(block, eye() * (2.0 / (1.0 + bound)), 6, inv_ref)
    for copy in copies[1:]:
        copy.wait()
    rhs = jnp.concatenate([left[i] for i in range(left.shape[0])] + [source[...]], axis=1)
    work = dot(inv_ref[...], rhs)
    spread(work_ref, 0, work)
    spread(first_ref, 0, tdot(right[0], work))
    spread(second_ref, 0, tdot(right[1], work))


def leaf(diag_blocks, left_bases, sources, right_bases):
    shapes = (diag_blocks.shape, left_bases.shape, sources.shape, (2,) + right_bases.shape[1:])
    return pl.pallas_call(
        leaf_kernel,
        out_shape=(jax.ShapeDtypeStruct((10, N, N), jnp.float32), blocks(10), blocks(10)),
        in_specs=[pl.BlockSpec(memory_space=pltpu.HBM)] * 4,
        scratch_shapes=[pltpu.VMEM(shape, jnp.float32) for shape in shapes]
        + [pltpu.SemaphoreType.DMA((4,)), pltpu.VMEM((N, N), jnp.float32)],
        compiler_params=pltpu.CompilerParams(vmem_limit_bytes=125 << 19),
        name="leaf",
    )(diag_blocks, left_bases, sources, right_bases)


def solve(level, own_g, other_g, rest, inv_ref):
    matrix = eye() - dot(other_g, own_g)
    start = general_start(matrix)
    own_p, other_p = rest()
    right = other_p - dot(other_g, own_p)
    invert(matrix, start, ROUNDS[level], inv_ref)
    return own_p, dot(inv_ref[...], right)


def pair_body(flag_ref, fetches, outs, inv_ref):
    own, other = (fetch.need() for fetch in fetches)
    count = own.shape[0]
    own_p, coef = solve(0, own[0], other[0], lambda: (wide(own, 1, count), wide(other, 1, count)), inv_ref)
    outs[0][...] = coef
    outs[1][...] = own_p - dot(own[0], coef)


def pair_apply_body(flag_ref, fetches, outs):
    work, coef = (fetch.need() for fetch in fetches)
    spread(outs[0], 0, wide(work, 1, work.shape[0]) - dot(work[0], coef[...]))


def merge_body(flag_ref, fetches, outs):
    coef_f, other_coef_f, own_f, other_f = fetches
    coef, other_coef, own, other = (fetch.need() for fetch in fetches)
    count = own.shape[0]
    merged = wide(own, 1, count) + wide(other, 1, count) - dot(own[0], coef[...]) - dot(other[0], other_coef[...])
    put_flat(outs[0], 0, merged)
    rows = outs[1].shape[0]
    outs[1][...] = outs[0][pl.ds(pl.multiple_of(flag_ref[0] * rows, 8), rows)]


def join(flag, mine_f, swapped_f, full_ref):
    rows = mine_f.buffer.shape[0]
    full_ref[pl.ds(pl.multiple_of(flag * rows, 8), rows)] = mine_f.need()[...]
    full_ref[pl.ds(pl.multiple_of((1 - flag) * rows, 8), rows)] = swapped_f.need()[...]
    return full_ref


def finish(level, own_g, other_g, panels, work_f, right_f, outs, inv_ref):
    work, right = work_f.need(), right_f.need()
    count = work.shape[0]
    _, coef = solve(level, own_g, other_g, panels, inv_ref)
    later = wide(work, 1, count) - dot(work[0], coef)
    for k in range(right.shape[0]):
        spread(outs[1], k * (count - 1), tdot(right[k], later))
    spread(outs[0], 0, later)


def quad_body(flag_ref, fetches, outs, inv_ref, full_ref):
    own_f, mine_f, swapped_f, work_f, right_f = fetches
    count = work_f.buffer.shape[0]
    other = join(flag_ref[0], mine_f, swapped_f, full_ref)
    own = own_f.need()

    def panels():
        return flat_wide(own, 1, count), flat_wide(other, 1, count)

    finish(1, own[:N], other[:N], panels, work_f, right_f, outs, inv_ref)


def level_body(level, flag_ref, fetches, outs, inv_ref):
    both_f, work_f, right_f = fetches
    count = work_f.buffer.shape[0]
    half = flag_ref[level]
    rows = both_f.buffer.shape[2]
    lead = -(-N // rows)
    first = both_f.need(1)
    own_g = first[:lead, half].reshape(lead * rows, N)[:N]
    other_g = first[:lead, 1 - half].reshape(lead * rows, N)[:N]

    def panels():
        both = both_f.need()
        return tuple(
            side([value[i] for i in range(1, count)])
            for value in (both[:, half].reshape(count, N, N), both[:, 1 - half].reshape(count, N, N))
        )

    finish(level, own_g, other_g, panels, work_f, right_f, outs, inv_ref)


def front_step(level, own_g, other_g, own, other, coef_ref, inv_ref):
    count = 10 - level
    readers = []

    def rest():
        readers.extend([own(), other()])
        return tuple(side([read(i) for i in range(1, count)]) for read in readers)

    own_p, coef = solve(level, own_g, other_g, rest, inv_ref)
    spread(coef_ref, 0, coef)
    other_coef = own_p - dot(own_g, coef)
    mine, yours = readers
    for base in range(count, count * (count - 1), count):
        both = side([mine(base + i) + yours(base + i) for i in range(1, count)])
        yield both - dot(mine(base), coef) - dot(yours(base), other_coef)


def stacked_reader(fetch):
    ref = fetch.need()
    return lambda i: ref[i]


def core_body(flag_ref, fetches, outs, inv_ref):
    own_f, other_f = fetches
    own_g, other_g = own_f.need(1)[0], other_f.need(1)[0]
    readers = [lambda fetch=fetch: stacked_reader(fetch) for fetch in fetches]
    for k, merged in enumerate(front_step(5, own_g, other_g, *readers, outs[0], inv_ref)):
        put_flat(outs[1], 4 * k, merged)
    rows = outs[2].shape[0]
    outs[2][...] = outs[1][pl.ds(pl.multiple_of(flag_ref[5] * rows, 8), rows)]


def joined_body(flag_ref, fetches, outs, inv_ref, full_ref):
    own_f, mine_f, swapped_f = fetches
    other = join(flag_ref[5], mine_f, swapped_f, full_ref)
    own = own_f.need()
    readers = [lambda ref=ref: (lambda i: ref[i * N : (i + 1) * N]) for ref in (own, other)]
    for k, merged in enumerate(front_step(6, own[:N], other[:N], *readers, outs[0], inv_ref)):
        spread(outs[1], 3 * k, merged)


def front_body(flag_ref, fetches, outs, inv_ref):
    own_f, other_f = fetches
    own_g, other_g = own_f.need(1)[0], other_f.need(1)[0]
    readers = [lambda fetch=fetch: stacked_reader(fetch) for fetch in fetches]
    for k, merged in enumerate(front_step(7, own_g, other_g, *readers, outs[0], inv_ref)):
        spread(outs[1], 2 * k, merged)


def last_body(flag_ref, fetches, outs, inv_ref):
    own_f, other_f, work_f = fetches
    own_g, other_g = own_f.need()[0], other_f.need()[0]

    def rest():
        work_f.need()
        return own_f.buffer[1], other_f.buffer[1]

    _, coef = solve(8, own_g, other_g, rest, inv_ref)
    outs[0][...] = work_f.buffer[1] - dot(work_f.buffer[0], coef)


def apply_body(flag_ref, fetches, outs):
    work, coef = (fetch.need() for fetch in fetches)
    count = work.shape[0]
    spread(outs[0], 0, wide(work, 1, count) - dot(work[0], wide(coef, 0, count - 1)))


def blocks(count):
    return pltpu.VMEM((count, N, N), jnp.float32)


def flat(rows, cols=N):
    return pltpu.VMEM((rows, cols), jnp.float32)


def partner(value, bit):
    return lax.ppermute(value, "b%d" % bit, [(0, 1), (1, 0)])


def exchange(value, names):
    return lax.all_to_all(value, names, 0, 0)


def tie(*values):
    return lax.optimization_barrier(values)


def half_sums(panel, level):
    size = 2 ** (level + 1)
    rows = panel.shape[0] * N // size
    names = axes(0, level + 1)
    pieces = exchange(panel.reshape(size, rows, N), names)
    sums = pieces.reshape(2, size // 2, rows, N).sum(axis=1)
    return exchange(jnp.broadcast_to(sums[None], (size, 2, rows, N)), names)


def total(panel, level):
    count = panel.shape[0]
    size = 2**level
    rows = count * N // size
    names = axes(0, level)
    pieces = exchange(panel.reshape(size, rows, N), names)
    part = pieces.sum(axis=0)
    return exchange(jnp.broadcast_to(part[None], (size, rows, N)), names).reshape(count, N, N)


def per_device(diag_blocks, left_bases, right_bases, sources):
    levels = left_bases.shape[0]
    targets = levels + 1
    flags = jnp.stack([lax.axis_index("b%d" % bit) for bit in range(BITS)]).astype(jnp.int32)
    done = []

    def some_right(low, high):
        return (right_bases, low, (0, high - low))

    work, first, second = leaf(diag_blocks, left_bases, sources, right_bases)
    first_other = partner(first, 0)
    second, first_other = tie(second, first_other)
    second_other = partner(second, 0)
    done.append(work[0])
    coef, other_coef = call(pair_body, "pair", (flat(N, 9 * N), flat(N, 9 * N)), first, first_other)
    front, part = call(
        merge_body, "merge", (flat(9 * N), flat(9 * N // 2)), coef, other_coef, second, second_other, flags=flags, inverse=False
    )
    mine = partner(part, 1)
    work = call(pair_apply_body, "apply0", blocks(9), work, coef, inverse=False)
    done.append(work[0])
    mine, work = tie(mine, work)
    swapped = partner(mine, 0)
    work, panel = call(
        quad_body, "quad", (blocks(8), blocks(8)), front, mine, swapped, work, some_right(2, 3), flags=flags, full=9 * N
    )
    done.append(work[0])

    for level in range(2, TOP):
        count = targets - level
        both = half_sums(panel, level)
        size, _, piece, _ = both.shape
        rows = 1 if level + 1 < TOP else levels - TOP

        def body(*refs, level=level):
            level_body(level, *refs)

        work, panel = call(
            body,
            "level%d" % level,
            (blocks(count - 1), blocks(rows * (count - 1))),
            (both, 0, (0, -(-N // piece), size)),
            work,
            some_right(level + 1, level + 1 + rows),
            flags=flags,
        )
        done.append(work[0])

    front = total(panel, TOP)
    other = partner(front, 5)
    coef, front, part = call(
        core_body, "front5", (blocks(4), flat(12 * N), flat(6 * N)), stacked_first(front), stacked_first(other), flags=flags
    )
    mine = partner(part, 6)
    work = call(apply_body, "apply5", blocks(4), work, coef, inverse=False)
    done.append(work[0])
    mine, work = tie(mine, work)
    swapped = partner(mine, 5)
    coef, front = call(joined_body, "front6", (blocks(3), blocks(6)), front, mine, swapped, flags=flags, full=12 * N)
    other = partner(front, 7)
    work = call(apply_body, "apply6", blocks(3), work, coef, inverse=False)
    done.append(work[0])
    other, work = tie(other, work)
    coef, front = call(front_body, "front7", (blocks(2), blocks(2)), stacked_first(front), stacked_first(other))
    other = partner(front, 8)
    work = call(apply_body, "apply7", blocks(2), work, coef, inverse=False)
    done.append(work[0])
    updated = jnp.stack(done)
    other, work, updated = tie(other, work, updated)
    out = call(last_body, "front8", flat(N), front, other, work)
    return updated, out


def solution(mesh):
    fine = Mesh(mesh.devices.reshape((2,) * BITS), NAMES)
    rows = P(NAMES, None)
    stacked = P(None, NAMES, None)
    return jax.shard_map(
        per_device,
        mesh=fine,
        in_specs=(rows, stacked, stacked, rows),
        out_specs=(stacked, rows),
        check_vma=False,
    )
```

```python
import jax
import jax.numpy as jnp
from jax import lax
from jax.experimental import pallas as pl
from jax.experimental.pallas import tpu as pltpu
from jax.sharding import Mesh, PartitionSpec as P

HI = lax.Precision.HIGHEST
BITS = 9
NAMES = tuple("b%d" % bit for bit in reversed(range(BITS)))
TOP = 5
STAGGER = 3000
ROUNDS = (9, 7, 6, 6, 5, 5, 5, 5, 5)
N = 128


def axes(low, high):
    return tuple("b%d" % bit for bit in reversed(range(low, high)))


def exact(a, b):
    return jnp.dot(a, b, precision=HI, preferred_element_type=jnp.float32)


def parts(value):
    high = value.astype(jnp.bfloat16)
    return high, (value - high.astype(jnp.float32)).astype(jnp.bfloat16)


def dot(a, b):
    a_high, a_low = parts(a)
    b_high, b_low = parts(b)

    def one(x, y):
        return jnp.dot(x, y, preferred_element_type=jnp.float32)

    return one(a_high, b_high) + (one(a_high, b_low) + one(a_low, b_high))


def tdot(a, b):
    return dot(a.T, b)


def quick(a, b):
    return jnp.dot(a.astype(jnp.bfloat16), b.astype(jnp.bfloat16), preferred_element_type=jnp.float32)


def eye():
    row = lax.broadcasted_iota(jnp.int32, (N, N), 0)
    col = lax.broadcasted_iota(jnp.int32, (N, N), 1)
    return (row == col).astype(jnp.float32)


def wide(ref, first, last):
    return jnp.concatenate([ref[i] for i in range(first, last)], axis=1)


def invert(matrix, start, rounds, out_ref):
    one = eye()
    value = start
    for _ in range(rounds):
        value = value + quick(value, one - quick(matrix, value))
    for product in (dot, exact):
        rest = one - product(matrix, value)
        value = value + quick(value, rest)
    out_ref[...] = value
    left = jnp.sum(rest * rest)

    @pl.when(jnp.logical_not(left < 1e-6))
    def _():
        out_ref[...] = jnp.where(left < 0.25, value, start)

        def more(state):
            step, left = state
            return jnp.logical_and(step < 60, jnp.logical_not(left < 1e-9))

        def body(state):
            step, _ = state
            now = out_ref[...]
            rest = eye() - exact(matrix, now)
            out_ref[...] = now + exact(now, rest)
            return step + 1, jnp.sum(rest * rest)

        lax.while_loop(more, body, (jnp.int32(0), jnp.float32(1.0)))


def general_start(matrix):
    size = jnp.abs(matrix)
    by_col = jnp.max(jnp.sum(size, axis=0, keepdims=True), axis=1, keepdims=True)
    by_row = jnp.max(jnp.sum(size, axis=1, keepdims=True), axis=0, keepdims=True)
    return matrix.T * (1.9 / (by_col * by_row))


def spread(ref, base, value):
    for i in range(value.shape[1] // N):
        ref[base + i] = value[:, i * N : (i + 1) * N]


def side(blocks):
    return jnp.concatenate(blocks, axis=1)


class Operand:
    def __init__(self, ref):
        self.buffer = ref

    def need(self, pieces=None):
        return self.buffer


def call(body, name, outs, *args, flags=None, full=0, inverse=True):
    arrays = [pltpu.with_memory_space_constraint(arg[0] if isinstance(arg, tuple) else arg, pltpu.VMEM) for arg in args]
    count = len(arrays)
    scratch = []
    if inverse:
        scratch.append(pltpu.VMEM((N, N), jnp.float32))
    if full:
        scratch.append(pltpu.VMEM((full, N), jnp.float32))
    results = outs if isinstance(outs, tuple) else (outs,)

    def kernel(*refs):
        flag_ref = None
        if flags is not None:
            flag_ref, refs = refs[0], refs[1:]
        operands = []
        for arg, ref in zip(args, refs[:count]):
            if isinstance(arg, tuple):
                ref = ref.at[pl.ds(arg[1], arg[2][-1])]
            operands.append(Operand(ref))
        refs = refs[count:]
        body(flag_ref, operands, refs[: len(results)], *refs[len(results) :])

    specs = [pl.BlockSpec(memory_space=pltpu.VMEM) for _ in arrays]
    if flags is not None:
        specs = [pl.BlockSpec(memory_space=pltpu.SMEM)] + specs
        arrays = [flags] + arrays
    params = pltpu.CompilerParams(vmem_limit_bytes=16 << 20)
    return pl.pallas_call(
        kernel, out_shape=outs, in_specs=specs, scratch_shapes=scratch, compiler_params=params, name=name
    )(*arrays)


def stacked_first(array):
    return (array, 0, (0, 1, array.shape[0]))


def flat_wide(ref, first, last):
    return side([ref[i * N : (i + 1) * N] for i in range(first, last)])


def put_flat(ref, base, value):
    for i in range(value.shape[1] // N):
        ref[(base + i) * N : (base + i + 1) * N] = value[:, i * N : (i + 1) * N]


def leaf_kernel(flag_ref, diag_any, left_any, source_any, right_any, work_ref, first_ref, second_ref, diag, left, source, right, sems, inv_ref):
    rows = right.shape[0]
    pairs = ((diag_any, diag), (left_any, left), (source_any, source), (right_any.at[pl.ds(0, rows)], right))
    copies = [pltpu.make_async_copy(*pair, sems.at[i]) for i, pair in enumerate(pairs)]
    for copy in copies:
        copy.start()
    copies[0].wait()
    block = diag[...]
    bound = jnp.max(jnp.sum(jnp.abs(block), axis=0, keepdims=True), axis=1, keepdims=True)
    invert(block, eye() * (2.0 / (1.0 + bound)), 6, inv_ref)
    for copy in copies[1:]:
        copy.wait()
    rhs = jnp.concatenate([left[i] for i in range(left.shape[0])] + [source[...]], axis=1)
    work = dot(inv_ref[...], rhs)
    spread(work_ref, 0, work)
    spread(first_ref, 0, tdot(right[0], work))
    spread(second_ref, 0, tdot(right[1], work))

    @pl.when(flag_ref[5] == 0)
    def _():
        pl.delay(STAGGER)


def leaf(flags, diag_blocks, left_bases, sources, right_bases):
    shapes = (diag_blocks.shape, left_bases.shape, sources.shape, (2,) + right_bases.shape[1:])
    return pl.pallas_call(
        leaf_kernel,
        out_shape=(jax.ShapeDtypeStruct((10, N, N), jnp.float32), blocks(10), blocks(10)),
        in_specs=[pl.BlockSpec(memory_space=pltpu.SMEM)] + [pl.BlockSpec(memory_space=pltpu.HBM)] * 4,
        scratch_shapes=[pltpu.VMEM(shape, jnp.float32) for shape in shapes]
        + [pltpu.SemaphoreType.DMA((4,)), pltpu.VMEM((N, N), jnp.float32)],
        compiler_params=pltpu.CompilerParams(vmem_limit_bytes=125 << 19),
        name="leaf",
    )(flags, diag_blocks, left_bases, sources, right_bases)


def solve(level, own_g, other_g, rest, inv_ref):
    matrix = eye() - dot(other_g, own_g)
    start = general_start(matrix)
    own_p, other_p = rest()
    right = other_p - dot(other_g, own_p)
    invert(matrix, start, ROUNDS[level], inv_ref)
    return own_p, dot(inv_ref[...], right)


def pair_body(flag_ref, fetches, outs, inv_ref):
    own, other = (fetch.need() for fetch in fetches)
    count = own.shape[0]
    own_p, coef = solve(0, own[0], other[0], lambda: (wide(own, 1, count), wide(other, 1, count)), inv_ref)
    outs[0][...] = coef
    outs[1][...] = own_p - dot(own[0], coef)


def pair_apply_body(flag_ref, fetches, outs):
    work, coef = (fetch.need() for fetch in fetches)
    spread(outs[0], 0, wide(work, 1, work.shape[0]) - dot(work[0], coef[...]))


def merge_body(flag_ref, fetches, outs):
    coef_f, other_coef_f, own_f, other_f = fetches
    coef, other_coef, own, other = (fetch.need() for fetch in fetches)
    count = own.shape[0]
    merged = wide(own, 1, count) + wide(other, 1, count) - dot(own[0], coef[...]) - dot(other[0], other_coef[...])
    put_flat(outs[0], 0, merged)
    rows = outs[1].shape[0]
    outs[1][...] = outs[0][pl.ds(pl.multiple_of(flag_ref[0] * rows, 8), rows)]


def join(flag, mine_f, swapped_f, full_ref):
    rows = mine_f.buffer.shape[0]
    full_ref[pl.ds(pl.multiple_of(flag * rows, 8), rows)] = mine_f.need()[...]
    full_ref[pl.ds(pl.multiple_of((1 - flag) * rows, 8), rows)] = swapped_f.need()[...]
    return full_ref


def finish(level, own_g, other_g, panels, work_f, right_f, outs, inv_ref):
    work, right = work_f.need(), right_f.need()
    count = work.shape[0]
    _, coef = solve(level, own_g, other_g, panels, inv_ref)
    later = wide(work, 1, count) - dot(work[0], coef)
    for k in range(right.shape[0]):
        spread(outs[1], k * (count - 1), tdot(right[k], later))
    spread(outs[0], 0, later)


def quad_body(flag_ref, fetches, outs, inv_ref, full_ref):
    own_f, mine_f, swapped_f, work_f, right_f = fetches
    count = work_f.buffer.shape[0]
    other = join(flag_ref[0], mine_f, swapped_f, full_ref)
    own = own_f.need()

    def panels():
        return flat_wide(own, 1, count), flat_wide(other, 1, count)

    finish(1, own[:N], other[:N], panels, work_f, right_f, outs, inv_ref)


def level_body(level, flag_ref, fetches, outs, inv_ref):
    both_f, work_f, right_f = fetches
    count = work_f.buffer.shape[0]
    half = flag_ref[level]
    rows = both_f.buffer.shape[2]
    lead = -(-N // rows)
    first = both_f.need(1)
    own_g = first[:lead, half].reshape(lead * rows, N)[:N]
    other_g = first[:lead, 1 - half].reshape(lead * rows, N)[:N]

    def panels():
        both = both_f.need()
        return tuple(
            side([value[i] for i in range(1, count)])
            for value in (both[:, half].reshape(count, N, N), both[:, 1 - half].reshape(count, N, N))
        )

    finish(level, own_g, other_g, panels, work_f, right_f, outs, inv_ref)


def front_step(level, own_g, other_g, own, other, coef_ref, inv_ref):
    count = 10 - level
    readers = []

    def rest():
        readers.extend([own(), other()])
        return tuple(side([read(i) for i in range(1, count)]) for read in readers)

    own_p, coef = solve(level, own_g, other_g, rest, inv_ref)
    spread(coef_ref, 0, coef)
    other_coef = own_p - dot(own_g, coef)
    mine, yours = readers
    for base in range(count, count * (count - 1), count):
        both = side([mine(base + i) + yours(base + i) for i in range(1, count)])
        yield both - dot(mine(base), coef) - dot(yours(base), other_coef)


def stacked_reader(fetch):
    ref = fetch.need()
    return lambda i: ref[i]


def core_body(flag_ref, fetches, outs, inv_ref):
    own_f, other_f = fetches
    own_g, other_g = own_f.need(1)[0], other_f.need(1)[0]
    readers = [lambda fetch=fetch: stacked_reader(fetch) for fetch in fetches]
    for k, merged in enumerate(front_step(5, own_g, other_g, *readers, outs[0], inv_ref)):
        put_flat(outs[1], 4 * k, merged)
    rows = outs[2].shape[0]
    outs[2][...] = outs[1][pl.ds(pl.multiple_of(flag_ref[5] * rows, 8), rows)]


def joined_body(flag_ref, fetches, outs, inv_ref, full_ref):
    own_f, mine_f, swapped_f = fetches
    other = join(flag_ref[5], mine_f, swapped_f, full_ref)
    own = own_f.need()
    readers = [lambda ref=ref: (lambda i: ref[i * N : (i + 1) * N]) for ref in (own, other)]
    for k, merged in enumerate(front_step(6, own[:N], other[:N], *readers, outs[0], inv_ref)):
        spread(outs[1], 3 * k, merged)


def front_body(flag_ref, fetches, outs, inv_ref):
    own_f, other_f = fetches
    own_g, other_g = own_f.need(1)[0], other_f.need(1)[0]
    readers = [lambda fetch=fetch: stacked_reader(fetch) for fetch in fetches]
    for k, merged in enumerate(front_step(7, own_g, other_g, *readers, outs[0], inv_ref)):
        spread(outs[1], 2 * k, merged)


def last_body(flag_ref, fetches, outs, inv_ref):
    own_f, other_f, work_f = fetches
    own_g, other_g = own_f.need()[0], other_f.need()[0]

    def rest():
        work_f.need()
        return own_f.buffer[1], other_f.buffer[1]

    _, coef = solve(8, own_g, other_g, rest, inv_ref)
    outs[0][...] = work_f.buffer[1] - dot(work_f.buffer[0], coef)


def apply_body(flag_ref, fetches, outs):
    work, coef = (fetch.need() for fetch in fetches)
    count = work.shape[0]
    spread(outs[0], 0, wide(work, 1, count) - dot(work[0], wide(coef, 0, count - 1)))


def blocks(count):
    return pltpu.VMEM((count, N, N), jnp.float32)


def flat(rows, cols=N):
    return pltpu.VMEM((rows, cols), jnp.float32)


def partner(value, bit):
    return lax.ppermute(value, "b%d" % bit, [(0, 1), (1, 0)])


def exchange(value, names):
    return lax.all_to_all(value, names, 0, 0)


def tie(*values):
    return lax.optimization_barrier(values)


def half_sums(panel, level):
    size = 2 ** (level + 1)
    rows = panel.shape[0] * N // size
    names = axes(0, level + 1)
    pieces = exchange(panel.reshape(size, rows, N), names)
    sums = pieces.reshape(2, size // 2, rows, N).sum(axis=1)
    return exchange(jnp.broadcast_to(sums[None], (size, 2, rows, N)), names)


def total(panel, level):
    count = panel.shape[0]
    size = 2**level
    rows = count * N // size
    names = axes(0, level)
    pieces = exchange(panel.reshape(size, rows, N), names)
    part = pieces.sum(axis=0)
    return exchange(jnp.broadcast_to(part[None], (size, rows, N)), names).reshape(count, N, N)


def per_device(diag_blocks, left_bases, right_bases, sources):
    levels = left_bases.shape[0]
    targets = levels + 1
    flags = jnp.stack([lax.axis_index("b%d" % bit) for bit in range(BITS)]).astype(jnp.int32)
    done = []

    def some_right(low, high):
        return (right_bases, low, (0, high - low))

    work, first, second = leaf(flags, diag_blocks, left_bases, sources, right_bases)
    first_other = partner(first, 0)
    second, first_other = tie(second, first_other)
    second_other = partner(second, 0)
    done.append(work[0])
    coef, other_coef = call(pair_body, "pair", (flat(N, 9 * N), flat(N, 9 * N)), first, first_other)
    front, part = call(
        merge_body, "merge", (flat(9 * N), flat(9 * N // 2)), coef, other_coef, second, second_other, flags=flags, inverse=False
    )
    mine = partner(part, 1)
    work = call(pair_apply_body, "apply0", blocks(9), work, coef, inverse=False)
    done.append(work[0])
    mine, work = tie(mine, work)
    swapped = partner(mine, 0)
    work, panel = call(
        quad_body, "quad", (blocks(8), blocks(8)), front, mine, swapped, work, some_right(2, 3), flags=flags, full=9 * N
    )
    done.append(work[0])

    for level in range(2, TOP):
        count = targets - level
        both = half_sums(panel, level)
        size, _, piece, _ = both.shape
        rows = 1 if level + 1 < TOP else levels - TOP

        def body(*refs, level=level):
            level_body(level, *refs)

        work, panel = call(
            body,
            "level%d" % level,
            (blocks(count - 1), blocks(rows * (count - 1))),
            (both, 0, (0, -(-N // piece), size)),
            work,
            some_right(level + 1, level + 1 + rows),
            flags=flags,
        )
        done.append(work[0])

    front = total(panel, TOP)
    other = partner(front, 5)
    coef, front, part = call(
        core_body, "front5", (blocks(4), flat(12 * N), flat(6 * N)), stacked_first(front), stacked_first(other), flags=flags
    )
    mine = partner(part, 6)
    work = call(apply_body, "apply5", blocks(4), work, coef, inverse=False)
    done.append(work[0])
    mine, work = tie(mine, work)
    swapped = partner(mine, 5)
    coef, front = call(joined_body, "front6", (blocks(3), blocks(6)), front, mine, swapped, flags=flags, full=12 * N)
    other = partner(front, 7)
    work = call(apply_body, "apply6", blocks(3), work, coef, inverse=False)
    done.append(work[0])
    other, work = tie(other, work)
    coef, front = call(front_body, "front7", (blocks(2), blocks(2)), stacked_first(front), stacked_first(other))
    other = partner(front, 8)
    work = call(apply_body, "apply7", blocks(2), work, coef, inverse=False)
    done.append(work[0])
    updated = jnp.stack(done)
    other, work, updated = tie(other, work, updated)
    out = call(last_body, "front8", flat(N), front, other, work)
    return updated, out


def solution(mesh):
    fine = Mesh(mesh.devices.reshape((2,) * BITS), NAMES)
    rows = P(NAMES, None)
    stacked = P(None, NAMES, None)
    return jax.shard_map(
        per_device,
        mesh=fine,
        in_specs=(rows, stacked, stacked, rows),
        out_specs=(stacked, rows),
        check_vma=False,
    )
```

```python
import jax
import jax.numpy as jnp
from jax import lax
from jax.experimental import pallas as pl
from jax.experimental.pallas import tpu as pltpu
from jax.sharding import Mesh, PartitionSpec as P

HI = lax.Precision.HIGHEST
BITS = 9
NAMES = tuple("b%d" % bit for bit in reversed(range(BITS)))
TOP = 5
STAGGER = 4000
ROUNDS = (9, 7, 6, 6, 5, 5, 5, 5, 5)
N = 128


def axes(low, high):
    return tuple("b%d" % bit for bit in reversed(range(low, high)))


def exact(a, b):
    return jnp.dot(a, b, precision=HI, preferred_element_type=jnp.float32)


def parts(value):
    high = value.astype(jnp.bfloat16)
    return high, (value - high.astype(jnp.float32)).astype(jnp.bfloat16)


def dot(a, b):
    a_high, a_low = parts(a)
    b_high, b_low = parts(b)

    def one(x, y):
        return jnp.dot(x, y, preferred_element_type=jnp.float32)

    return one(a_high, b_high) + (one(a_high, b_low) + one(a_low, b_high))


def tdot(a, b):
    return dot(a.T, b)


def quick(a, b):
    return jnp.dot(a.astype(jnp.bfloat16), b.astype(jnp.bfloat16), preferred_element_type=jnp.float32)


def eye():
    row = lax.broadcasted_iota(jnp.int32, (N, N), 0)
    col = lax.broadcasted_iota(jnp.int32, (N, N), 1)
    return (row == col).astype(jnp.float32)


def wide(ref, first, last):
    return jnp.concatenate([ref[i] for i in range(first, last)], axis=1)


def invert(matrix, start, rounds, out_ref):
    one = eye()
    value = start
    for _ in range(rounds):
        value = value + quick(value, one - quick(matrix, value))
    for product in (dot, exact):
        rest = one - product(matrix, value)
        value = value + quick(value, rest)
    out_ref[...] = value
    left = jnp.sum(rest * rest)

    @pl.when(jnp.logical_not(left < 1e-6))
    def _():
        out_ref[...] = jnp.where(left < 0.25, value, start)

        def more(state):
            step, left = state
            return jnp.logical_and(step < 60, jnp.logical_not(left < 1e-9))

        def body(state):
            step, _ = state
            now = out_ref[...]
            rest = eye() - exact(matrix, now)
            out_ref[...] = now + exact(now, rest)
            return step + 1, jnp.sum(rest * rest)

        lax.while_loop(more, body, (jnp.int32(0), jnp.float32(1.0)))


def general_start(matrix):
    size = jnp.abs(matrix)
    by_col = jnp.max(jnp.sum(size, axis=0, keepdims=True), axis=1, keepdims=True)
    by_row = jnp.max(jnp.sum(size, axis=1, keepdims=True), axis=0, keepdims=True)
    return matrix.T * (1.9 / (by_col * by_row))


def spread(ref, base, value):
    for i in range(value.shape[1] // N):
        ref[base + i] = value[:, i * N : (i + 1) * N]


def side(blocks):
    return jnp.concatenate(blocks, axis=1)


class Operand:
    def __init__(self, ref):
        self.buffer = ref

    def need(self, pieces=None):
        return self.buffer


def call(body, name, outs, *args, flags=None, full=0, inverse=True):
    arrays = [pltpu.with_memory_space_constraint(arg[0] if isinstance(arg, tuple) else arg, pltpu.VMEM) for arg in args]
    count = len(arrays)
    scratch = []
    if inverse:
        scratch.append(pltpu.VMEM((N, N), jnp.float32))
    if full:
        scratch.append(pltpu.VMEM((full, N), jnp.float32))
    results = outs if isinstance(outs, tuple) else (outs,)

    def kernel(*refs):
        flag_ref = None
        if flags is not None:
            flag_ref, refs = refs[0], refs[1:]
        operands = []
        for arg, ref in zip(args, refs[:count]):
            if isinstance(arg, tuple):
                ref = ref.at[pl.ds(arg[1], arg[2][-1])]
            operands.append(Operand(ref))
        refs = refs[count:]
        body(flag_ref, operands, refs[: len(results)], *refs[len(results) :])

    specs = [pl.BlockSpec(memory_space=pltpu.VMEM) for _ in arrays]
    if flags is not None:
        specs = [pl.BlockSpec(memory_space=pltpu.SMEM)] + specs
        arrays = [flags] + arrays
    params = pltpu.CompilerParams(vmem_limit_bytes=16 << 20)
    return pl.pallas_call(
        kernel, out_shape=outs, in_specs=specs, scratch_shapes=scratch, compiler_params=params, name=name
    )(*arrays)


def stacked_first(array):
    return (array, 0, (0, 1, array.shape[0]))


def flat_wide(ref, first, last):
    return side([ref[i * N : (i + 1) * N] for i in range(first, last)])


def put_flat(ref, base, value):
    for i in range(value.shape[1] // N):
        ref[(base + i) * N : (base + i + 1) * N] = value[:, i * N : (i + 1) * N]


def leaf_kernel(flag_ref, diag_any, left_any, source_any, right_any, work_ref, first_ref, second_ref, diag, left, source, right, sems, inv_ref):
    rows = right.shape[0]
    pairs = ((diag_any, diag), (left_any, left), (source_any, source), (right_any.at[pl.ds(0, rows)], right))
    copies = [pltpu.make_async_copy(*pair, sems.at[i]) for i, pair in enumerate(pairs)]
    for copy in copies:
        copy.start()
    copies[0].wait()
    block = diag[...]
    bound = jnp.max(jnp.sum(jnp.abs(block), axis=0, keepdims=True), axis=1, keepdims=True)
    invert(block, eye() * (2.0 / (1.0 + bound)), 6, inv_ref)
    for copy in copies[1:]:
        copy.wait()
    rhs = jnp.concatenate([left[i] for i in range(left.shape[0])] + [source[...]], axis=1)
    work = dot(inv_ref[...], rhs)
    spread(work_ref, 0, work)
    spread(first_ref, 0, tdot(right[0], work))
    spread(second_ref, 0, tdot(right[1], work))

    @pl.when(flag_ref[5] == 0)
    def _():
        pl.delay(STAGGER)


def leaf(flags, diag_blocks, left_bases, sources, right_bases):
    shapes = (diag_blocks.shape, left_bases.shape, sources.shape, (2,) + right_bases.shape[1:])
    return pl.pallas_call(
        leaf_kernel,
        out_shape=(jax.ShapeDtypeStruct((10, N, N), jnp.float32), blocks(10), blocks(10)),
        in_specs=[pl.BlockSpec(memory_space=pltpu.SMEM)] + [pl.BlockSpec(memory_space=pltpu.HBM)] * 4,
        scratch_shapes=[pltpu.VMEM(shape, jnp.float32) for shape in shapes]
        + [pltpu.SemaphoreType.DMA((4,)), pltpu.VMEM((N, N), jnp.float32)],
        compiler_params=pltpu.CompilerParams(vmem_limit_bytes=125 << 19),
        name="leaf",
    )(flags, diag_blocks, left_bases, sources, right_bases)


def solve(level, own_g, other_g, rest, inv_ref):
    matrix = eye() - dot(other_g, own_g)
    start = general_start(matrix)
    own_p, other_p = rest()
    right = other_p - dot(other_g, own_p)
    invert(matrix, start, ROUNDS[level], inv_ref)
    return own_p, dot(inv_ref[...], right)


def pair_body(flag_ref, fetches, outs, inv_ref):
    own, other = (fetch.need() for fetch in fetches)
    count = own.shape[0]
    own_p, coef = solve(0, own[0], other[0], lambda: (wide(own, 1, count), wide(other, 1, count)), inv_ref)
    outs[0][...] = coef
    outs[1][...] = own_p - dot(own[0], coef)


def pair_apply_body(flag_ref, fetches, outs):
    work, coef = (fetch.need() for fetch in fetches)
    spread(outs[0], 0, wide(work, 1, work.shape[0]) - dot(work[0], coef[...]))


def merge_body(flag_ref, fetches, outs):
    coef_f, other_coef_f, own_f, other_f = fetches
    coef, other_coef, own, other = (fetch.need() for fetch in fetches)
    count = own.shape[0]
    merged = wide(own, 1, count) + wide(other, 1, count) - dot(own[0], coef[...]) - dot(other[0], other_coef[...])
    put_flat(outs[0], 0, merged)
    rows = outs[1].shape[0]
    outs[1][...] = outs[0][pl.ds(pl.multiple_of(flag_ref[0] * rows, 8), rows)]


def join(flag, mine_f, swapped_f, full_ref):
    rows = mine_f.buffer.shape[0]
    full_ref[pl.ds(pl.multiple_of(flag * rows, 8), rows)] = mine_f.need()[...]
    full_ref[pl.ds(pl.multiple_of((1 - flag) * rows, 8), rows)] = swapped_f.need()[...]
    return full_ref


def finish(level, own_g, other_g, panels, work_f, right_f, outs, inv_ref):
    work, right = work_f.need(), right_f.need()
    count = work.shape[0]
    _, coef = solve(level, own_g, other_g, panels, inv_ref)
    later = wide(work, 1, count) - dot(work[0], coef)
    for k in range(right.shape[0]):
        spread(outs[1], k * (count - 1), tdot(right[k], later))
    spread(outs[0], 0, later)


def quad_body(flag_ref, fetches, outs, inv_ref, full_ref):
    own_f, mine_f, swapped_f, work_f, right_f = fetches
    count = work_f.buffer.shape[0]
    other = join(flag_ref[0], mine_f, swapped_f, full_ref)
    own = own_f.need()

    def panels():
        return flat_wide(own, 1, count), flat_wide(other, 1, count)

    finish(1, own[:N], other[:N], panels, work_f, right_f, outs, inv_ref)


def level_body(level, flag_ref, fetches, outs, inv_ref):
    both_f, work_f, right_f = fetches
    count = work_f.buffer.shape[0]
    half = flag_ref[level]
    rows = both_f.buffer.shape[2]
    lead = -(-N // rows)
    first = both_f.need(1)
    own_g = first[:lead, half].reshape(lead * rows, N)[:N]
    other_g = first[:lead, 1 - half].reshape(lead * rows, N)[:N]

    def panels():
        both = both_f.need()
        return tuple(
            side([value[i] for i in range(1, count)])
            for value in (both[:, half].reshape(count, N, N), both[:, 1 - half].reshape(count, N, N))
        )

    finish(level, own_g, other_g, panels, work_f, right_f, outs, inv_ref)


def front_step(level, own_g, other_g, own, other, coef_ref, inv_ref):
    count = 10 - level
    readers = []

    def rest():
        readers.extend([own(), other()])
        return tuple(side([read(i) for i in range(1, count)]) for read in readers)

    own_p, coef = solve(level, own_g, other_g, rest, inv_ref)
    spread(coef_ref, 0, coef)
    other_coef = own_p - dot(own_g, coef)
    mine, yours = readers
    for base in range(count, count * (count - 1), count):
        both = side([mine(base + i) + yours(base + i) for i in range(1, count)])
        yield both - dot(mine(base), coef) - dot(yours(base), other_coef)


def stacked_reader(fetch):
    ref = fetch.need()
    return lambda i: ref[i]


def core_body(flag_ref, fetches, outs, inv_ref):
    own_f, other_f = fetches
    own_g, other_g = own_f.need(1)[0], other_f.need(1)[0]
    readers = [lambda fetch=fetch: stacked_reader(fetch) for fetch in fetches]
    for k, merged in enumerate(front_step(5, own_g, other_g, *readers, outs[0], inv_ref)):
        put_flat(outs[1], 4 * k, merged)
    rows = outs[2].shape[0]
    outs[2][...] = outs[1][pl.ds(pl.multiple_of(flag_ref[5] * rows, 8), rows)]


def joined_body(flag_ref, fetches, outs, inv_ref, full_ref):
    own_f, mine_f, swapped_f = fetches
    other = join(flag_ref[5], mine_f, swapped_f, full_ref)
    own = own_f.need()
    readers = [lambda ref=ref: (lambda i: ref[i * N : (i + 1) * N]) for ref in (own, other)]
    for k, merged in enumerate(front_step(6, own[:N], other[:N], *readers, outs[0], inv_ref)):
        spread(outs[1], 3 * k, merged)


def front_body(flag_ref, fetches, outs, inv_ref):
    own_f, other_f = fetches
    own_g, other_g = own_f.need(1)[0], other_f.need(1)[0]
    readers = [lambda fetch=fetch: stacked_reader(fetch) for fetch in fetches]
    for k, merged in enumerate(front_step(7, own_g, other_g, *readers, outs[0], inv_ref)):
        spread(outs[1], 2 * k, merged)


def last_body(flag_ref, fetches, outs, inv_ref):
    own_f, other_f, work_f = fetches
    own_g, other_g = own_f.need()[0], other_f.need()[0]

    def rest():
        work_f.need()
        return own_f.buffer[1], other_f.buffer[1]

    _, coef = solve(8, own_g, other_g, rest, inv_ref)
    outs[0][...] = work_f.buffer[1] - dot(work_f.buffer[0], coef)


def apply_body(flag_ref, fetches, outs):
    work, coef = (fetch.need() for fetch in fetches)
    count = work.shape[0]
    spread(outs[0], 0, wide(work, 1, count) - dot(work[0], wide(coef, 0, count - 1)))


def blocks(count):
    return pltpu.VMEM((count, N, N), jnp.float32)


def flat(rows, cols=N):
    return pltpu.VMEM((rows, cols), jnp.float32)


def partner(value, bit):
    return lax.ppermute(value, "b%d" % bit, [(0, 1), (1, 0)])


def exchange(value, names):
    return lax.all_to_all(value, names, 0, 0)


def tie(*values):
    return lax.optimization_barrier(values)


def half_sums(panel, level):
    size = 2 ** (level + 1)
    rows = panel.shape[0] * N // size
    names = axes(0, level + 1)
    pieces = exchange(panel.reshape(size, rows, N), names)
    sums = pieces.reshape(2, size // 2, rows, N).sum(axis=1)
    return exchange(jnp.broadcast_to(sums[None], (size, 2, rows, N)), names)


def total(panel, level):
    count = panel.shape[0]
    size = 2**level
    rows = count * N // size
    names = axes(0, level)
    pieces = exchange(panel.reshape(size, rows, N), names)
    part = pieces.sum(axis=0)
    return exchange(jnp.broadcast_to(part[None], (size, rows, N)), names).reshape(count, N, N)


def per_device(diag_blocks, left_bases, right_bases, sources):
    levels = left_bases.shape[0]
    targets = levels + 1
    flags = jnp.stack([lax.axis_index("b%d" % bit) for bit in range(BITS)]).astype(jnp.int32)
    done = []

    def some_right(low, high):
        return (right_bases, low, (0, high - low))

    work, first, second = leaf(flags, diag_blocks, left_bases, sources, right_bases)
    first_other = partner(first, 0)
    second, first_other = tie(second, first_other)
    second_other = partner(second, 0)
    done.append(work[0])
    coef, other_coef = call(pair_body, "pair", (flat(N, 9 * N), flat(N, 9 * N)), first, first_other)
    front, part = call(
        merge_body, "merge", (flat(9 * N), flat(9 * N // 2)), coef, other_coef, second, second_other, flags=flags, inverse=False
    )
    mine = partner(part, 1)
    work = call(pair_apply_body, "apply0", blocks(9), work, coef, inverse=False)
    done.append(work[0])
    mine, work = tie(mine, work)
    swapped = partner(mine, 0)
    work, panel = call(
        quad_body, "quad", (blocks(8), blocks(8)), front, mine, swapped, work, some_right(2, 3), flags=flags, full=9 * N
    )
    done.append(work[0])

    for level in range(2, TOP):
        count = targets - level
        both = half_sums(panel, level)
        size, _, piece, _ = both.shape
        rows = 1 if level + 1 < TOP else levels - TOP

        def body(*refs, level=level):
            level_body(level, *refs)

        work, panel = call(
            body,
            "level%d" % level,
            (blocks(count - 1), blocks(rows * (count - 1))),
            (both, 0, (0, -(-N // piece), size)),
            work,
            some_right(level + 1, level + 1 + rows),
            flags=flags,
        )
        done.append(work[0])

    front = total(panel, TOP)
    other = partner(front, 5)
    coef, front, part = call(
        core_body, "front5", (blocks(4), flat(12 * N), flat(6 * N)), stacked_first(front), stacked_first(other), flags=flags
    )
    mine = partner(part, 6)
    work = call(apply_body, "apply5", blocks(4), work, coef, inverse=False)
    done.append(work[0])
    mine, work = tie(mine, work)
    swapped = partner(mine, 5)
    coef, front = call(joined_body, "front6", (blocks(3), blocks(6)), front, mine, swapped, flags=flags, full=12 * N)
    other = partner(front, 7)
    work = call(apply_body, "apply6", blocks(3), work, coef, inverse=False)
    done.append(work[0])
    other, work = tie(other, work)
    coef, front = call(front_body, "front7", (blocks(2), blocks(2)), stacked_first(front), stacked_first(other))
    other = partner(front, 8)
    work = call(apply_body, "apply7", blocks(2), work, coef, inverse=False)
    done.append(work[0])
    updated = jnp.stack(done)
    other, work, updated = tie(other, work, updated)
    out = call(last_body, "front8", flat(N), front, other, work)
    return updated, out


def solution(mesh):
    fine = Mesh(mesh.devices.reshape((2,) * BITS), NAMES)
    rows = P(NAMES, None)
    stacked = P(None, NAMES, None)
    return jax.shard_map(
        per_device,
        mesh=fine,
        in_specs=(rows, stacked, stacked, rows),
        out_specs=(stacked, rows),
        check_vma=False,
    )
```
